32 devices in a mesh: wrk: 8 (over z, y), firm: 4 (over x, core).
Axes of the slice: x: 2, y: 2, z: 4, core: 2. Of those that a mesh axis runs over, the one named last changes fastest.
Arguments:
- feat_wrk: float32 [4096, 64], P('wrk'), may hold values from -9 to 9
- feat_firm: float32 [64, 16384], P(None, 'firm'), may hold values from -12 to 12
- surplus: float32 [64, 64], replicated, may hold values from -0.125 to 1.125
- row_start: float32 [4096], P('wrk'), may hold values from -5 to 5
- col_start: float32 [16384], P('firm'), may hold values from -5 to 5
- row_mass: float32 [4096], P('wrk'), may hold values from -1.5 to 1.5
- col_mass: float32 [16384], P('firm'), may hold values from -1.5 to 1.5
- row_cot: float32 [4096], P('wrk'), may hold values from -5 to 5
- col_cot: float32 [16384], P('firm'), may hold values from -5 to 5
Outputs:
- grad_surplus: float32 [64, 64], replicated
- grad_row: float32 [4096], P('wrk')
- grad_col: float32 [16384], P('firm')
The draws below stay inside these ranges and needn't reach their ends.
All inputs are finite; a program needn't handle non-finite values.
Results may differ from the reference program's by a relative error of at most 0.0003.
Values sent between devices are 32-bit elements; how exact they have to be, the bound alone decides.
No kernel may reach another device: no remote copies, remote signals or barrier semaphores. Data moves between devices by JAX's collectives and lax.ppermute only.
A program may use at most 64 MiB of HBM per device.

```python
import math
import jax
import jax.numpy as jnp
from jax import lax

RANK = 64
ITERS = 3
ROWS = 4096
COLS = 16384


def firm_basis(key):
    folded = jax.random.fold_in(key, 7)
    return jax.random.truncated_normal(folded, -4.0, 4.0, (COLS, RANK), jnp.float32)


def draw_feat_firm(key, part):
    basis = firm_basis(key)
    scaling = jnp.exp(jax.random.uniform(jax.random.fold_in(key, 8), (COLS, 1), jnp.float32, math.log(0.33), math.log(3.0)))
    features = basis * scaling
    return features.T


def draw_feat_wrk(key, part):
    folded = jax.random.fold_in(key, 9)
    raw_rows = jax.random.truncated_normal(folded, -4.0, 4.0, (ROWS, RANK), jnp.float32)
    scaling = jnp.exp(jax.random.uniform(jax.random.fold_in(key, 10), (ROWS, 1), jnp.float32, math.log(0.33), math.log(3.0)))
    features = 0.15 * raw_rows * scaling
    return features


def draw_surplus(key, part):
    noise = jax.random.truncated_normal(jax.random.fold_in(key, 12), -4.0, 4.0, (RANK, RANK), jnp.float32)
    return jnp.eye(RANK, dtype=jnp.float32) + 0.03125 * noise


def levels(own_key, extent, pieces, least, high):
    gain = 1.0
    for position, parts in pieces:
        draws = jax.random.uniform(jax.random.fold_in(jax.random.fold_in(own_key, 6), position), (parts,), jnp.float32, least / len(pieces), high / len(pieces))
        gain = gain * jnp.repeat(jnp.exp(draws), extent[position] // parts).reshape((-1,) + (1,) * (len(extent) - 1 - position))
    return gain


def scatter_about(stream_key, extent, spread, most, shards=(), held_as=jnp.bfloat16):
    loudness = levels(stream_key, extent, shards, -0.22, 0.18) if shards else 1.0
    array = jax.random.normal(stream_key, extent, jnp.float32) * spread * loudness
    return jnp.minimum(jnp.maximum(array, -most), most).astype(held_as)


def setup_inputs(seed: int = 0) -> dict:
    streams_of = jax.random.split(jax.random.key(seed), 10)
    feat_wrk = draw_feat_wrk(jax.random.fold_in(streams_of[9], 71), 0)
    feat_firm = draw_feat_firm(jax.random.fold_in(streams_of[9], 71), 0)
    surplus = draw_surplus(jax.random.fold_in(streams_of[9], 71), 0)
    row_start = scatter_about(streams_of[3], (ROWS,), 1.0, 5.0, ((0, 8),), jnp.float32)
    col_start = scatter_about(streams_of[4], (COLS,), 1.0, 5.0, ((0, 4),), jnp.float32)
    row_mass = jnp.clip(jax.random.uniform(streams_of[5], (ROWS,), jnp.float32, -1.5, 1.5) * levels(streams_of[5], (ROWS,), ((0, 8),), -0.4, 0.0), -1.5, 1.5)
    col_mass = jnp.clip(jax.random.uniform(streams_of[6], (COLS,), jnp.float32, -1.5, 1.5) * levels(streams_of[6], (COLS,), ((0, 4),), -0.4, 0.0), -1.5, 1.5)
    row_cot = scatter_about(streams_of[7], (ROWS,), 1.0, 5.0, ((0, 8),), jnp.float32)
    col_cot = scatter_about(streams_of[8], (COLS,), 1.0, 5.0, ((0, 4),), jnp.float32)
    return {"feat_wrk": feat_wrk, "feat_firm": feat_firm, "surplus": surplus, "row_start": row_start, "col_start": col_start, "row_mass": row_mass, "col_mass": col_mass, "row_cot": row_cot, "col_cot": col_cot}


HIGHEST = lax.Precision.HIGHEST


def row_stat(mixed, firm_cols, col_shift):
    block_rows = math.gcd(ROWS, 256)
    row_blocks = mixed.reshape(ROWS // block_rows, block_rows, RANK)

    def one_block(block_mixed):
        scores = jnp.dot(block_mixed, firm_cols, precision=HIGHEST) - col_shift[None, :]
        largest = jnp.max(scores, axis=1)
        return largest + jnp.log(jnp.sum(jnp.exp(scores - largest[:, None]), axis=1))

    return lax.map(one_block, row_blocks).reshape(ROWS)


def col_stat(mixed, firm_cols, row_shift):
    block_cols = math.gcd(COLS, 256)
    col_blocks = firm_cols.reshape(RANK, COLS // block_cols, block_cols).transpose(1, 0, 2)

    def one_block(block_firm):
        scores = jnp.dot(mixed, block_firm, precision=HIGHEST) - row_shift[:, None]
        largest = jnp.max(scores, axis=0)
        return largest + jnp.log(jnp.sum(jnp.exp(scores - largest[None, :]), axis=0))

    return lax.map(one_block, col_blocks).reshape(COLS)


def col_adjoint(mixed, firm_cols, row_pot, col_log, col_weight):
    block_cols = math.gcd(COLS, 256)
    count_blocks = COLS // block_cols
    col_blocks = firm_cols.reshape(RANK, count_blocks, block_cols).transpose(1, 0, 2)
    log_blocks = col_log.reshape(count_blocks, block_cols)
    weight_blocks = col_weight.reshape(count_blocks, block_cols)

    def block_step(carry, items):
        grad_part, row_total = carry
        block_firm, block_log, block_weight = items
        scores = jnp.dot(mixed, block_firm, precision=HIGHEST) - row_pot[:, None]
        weights = jnp.exp(scores - block_log[None, :]) * block_weight[None, :]
        grad_part = grad_part + jnp.dot(weights, block_firm.T, precision=HIGHEST)
        return (grad_part, row_total + jnp.sum(weights, axis=1)), None

    start_state = (jnp.zeros((ROWS, RANK), jnp.float32), jnp.zeros((ROWS,), jnp.float32))
    (grad_part, row_total), unused = lax.scan(block_step, start_state, (col_blocks, log_blocks, weight_blocks))
    return grad_part, row_total


def row_adjoint(mixed, firm_cols, col_pot, row_log, row_weight):
    block_rows = math.gcd(ROWS, 256)
    count_blocks = ROWS // block_rows
    row_blocks = mixed.reshape(count_blocks, block_rows, RANK)
    log_blocks = row_log.reshape(count_blocks, block_rows)
    weight_blocks = row_weight.reshape(count_blocks, block_rows)

    def block_step(col_total, items):
        block_mixed, block_log, block_weight = items
        scores = jnp.dot(block_mixed, firm_cols, precision=HIGHEST) - col_pot[None, :]
        weights = jnp.exp(scores - block_log[:, None]) * block_weight[:, None]
        grad_rows = jnp.dot(weights, firm_cols.T, precision=HIGHEST)
        return col_total + jnp.sum(weights, axis=0), grad_rows

    col_total, grad_blocks = lax.scan(block_step, jnp.zeros((COLS,), jnp.float32), (row_blocks, log_blocks, weight_blocks))
    return grad_blocks.reshape(ROWS, RANK), col_total


def reference(feat_wrk, feat_firm, surplus, row_start, col_start, row_mass, col_mass, row_cot, col_cot):
    mixed = jnp.dot(feat_wrk, surplus, precision=HIGHEST)
    row_pots = [row_start]
    col_pots = [col_start]
    row_logs = []
    col_logs = []
    for iteration in range(ITERS):
        row_log = row_stat(mixed, feat_firm, col_pots[-1])
        row_pots.append(0.5 * row_pots[-1] + 0.5 * (row_log - row_mass))
        col_log = col_stat(mixed, feat_firm, row_pots[-1])
        col_pots.append(0.5 * col_pots[-1] + 0.5 * (col_log - col_mass))
        row_logs.append(row_log)
        col_logs.append(col_log)
    row_bar = row_cot
    col_bar = col_cot
    grad_mixed = jnp.zeros((ROWS, RANK), jnp.float32)
    for iteration in reversed(range(ITERS)):
        grad_part, row_total = col_adjoint(mixed, feat_firm, row_pots[iteration + 1], col_logs[iteration], 0.5 * col_bar)
        grad_mixed = grad_mixed + grad_part
        row_bar = row_bar - row_total
        col_bar = 0.5 * col_bar
        grad_part, col_total = row_adjoint(mixed, feat_firm, col_pots[iteration], row_logs[iteration], 0.5 * row_bar)
        grad_mixed = grad_mixed + grad_part
        col_bar = col_bar - col_total
        row_bar = 0.5 * row_bar
    grad_surplus = jnp.dot(feat_wrk.T, grad_mixed, precision=HIGHEST)
    return grad_surplus, row_bar, col_bar
```

```python
import math

import jax
import jax.numpy as jnp
from jax import lax
from jax.experimental import pallas as pl
from jax.experimental.pallas import tpu as pltpu
from jax.sharding import PartitionSpec as P

ITERS = 3
LOG2E = 1.0 / math.log(2.0)
HIGHEST = lax.Precision.HIGHEST
LANES = 128
GROUP = 8
WHOLE = pl.BlockSpec(memory_space=pltpu.VMEM)
VMEM_LIMIT = 24 * 1024 * 1024


def tree(values, combine):
    values = list(values)
    while len(values) > 1:
        paired = [combine(values[i], values[i + 1]) for i in range(0, len(values) - 1, 2)]
        if len(values) % 2:
            paired.append(values[-1])
        values = paired
    return values[0]


def shape_of(*dims):
    return jax.ShapeDtypeStruct(dims, jnp.float32)


def call(kernel, name, outs, args, scratch=(), aliases=None):
    return pl.pallas_call(
        kernel,
        name=name,
        out_shape=outs,
        in_specs=[WHOLE] * len(args),
        out_specs=jax.tree.map(lambda _: WHOLE, outs),
        scratch_shapes=scratch,
        input_output_aliases=aliases or {},
        compiler_params=pltpu.CompilerParams(vmem_limit_bytes=VMEM_LIMIT),
    )(*args)


def lane(k):
    return pl.ds(k * LANES, LANES)


def lse_parts(parts):
    largest = tree(parts, jnp.maximum)
    return largest + jnp.log2(tree([jnp.exp2(p - largest) for p in parts], jnp.add))


def spread_rows(value, ref):
    for block in range(value.shape[0]):
        wide = jnp.broadcast_to(value[block : block + 1, :], (LANES, LANES))
        ref[pl.ds(block * LANES, LANES), :] = wide.T


def row_lse(s_ref, shift_ref, max_ref, sum_ref, out_ref):
    rows, cols = s_ref.shape
    tiles = cols // LANES

    def group_step(g, carry):
        r = pl.ds(g * GROUP, GROUP)
        terms = [s_ref[r, lane(k)] - shift_ref[k : k + 1, :] for k in range(tiles)]
        largest = tree(terms, jnp.maximum)
        max_ref[r, :] = largest
        sum_ref[r, :] = tree([jnp.exp2(t - largest) for t in terms], jnp.add)
        return carry

    lax.fori_loop(0, rows // GROUP, group_step, 0)
    for block in range(rows // LANES):
        b = pl.ds(block * LANES, LANES)
        maxes = max_ref[b, :].T
        sums = sum_ref[b, :].T
        largest = jnp.max(maxes, axis=0, keepdims=True)
        total = jnp.sum(sums * jnp.exp2(maxes - largest), axis=0, keepdims=True)
        out_ref[block : block + 1, :] = largest + jnp.log2(total)


def col_blocking(cols):
    tiles = cols // LANES
    width = math.gcd(tiles, 8)
    return width, tiles // width


def send_all(col_ref, out_ref):
    value = col_ref[...]
    for peer in range(out_ref.shape[0]):
        out_ref[peer] = value


def col_lse(s_ref, shift_ref, col_ref):
    rows, cols = s_ref.shape
    width, chunks = col_blocking(cols)
    per_step = math.gcd(rows // GROUP, 8)
    steps = rows // (GROUP * per_step)

    def chunk_step(c, carry):
        def terms_of(step, q):
            r = pl.ds(step * (GROUP * per_step) + q * GROUP, GROUP)
            shift = shift_ref[r, :]
            return [
                s_ref[r, pl.ds(c * (width * LANES) + k * LANES, LANES)] - shift
                for k in range(width)
            ]

        def max_step(step, maxes):
            for q in range(per_step):
                terms = terms_of(step, q)
                maxes = tuple(jnp.maximum(m, t) for m, t in zip(maxes, terms))
            return maxes

        low = jnp.full((GROUP, LANES), -jnp.inf, jnp.float32)
        maxes = lax.fori_loop(0, steps, max_step, (low,) * width)

        def sum_step(step, sums):
            for q in range(per_step):
                terms = terms_of(step, q)
                sums = tuple(s + jnp.exp2(t - m) for s, t, m in zip(sums, terms, maxes))
            return sums

        zero = jnp.zeros((GROUP, LANES), jnp.float32)
        sums = lax.fori_loop(0, steps, sum_step, (zero,) * width)
        for k in range(width):
            largest = jnp.max(maxes[k], axis=0, keepdims=True)
            total = jnp.sum(sums[k] * jnp.exp2(maxes[k] - largest), axis=0, keepdims=True)
            col_ref[pl.ds(c * width + k, 1), :] = largest + jnp.log2(total)
        return carry

    lax.fori_loop(0, chunks, chunk_step, 0)


def first_row_kernel(fw_ref, ff_ref, sp_ref, start_ref, s_ref, out_ref, cp_ref, rhs_ref, max_ref, sum_ref):
    rank, cols = ff_ref.shape
    mixed = lax.dot_general(
        sp_ref[...], fw_ref[...], (((0,), (1,)), ((), ())), precision=HIGHEST,
        preferred_element_type=jnp.float32,
    ) * LOG2E

    def split(value):
        first = value.astype(jnp.bfloat16)
        rest = value - first.astype(jnp.float32)
        second = rest.astype(jnp.bfloat16)
        third = (rest - second.astype(jnp.float32)).astype(jnp.bfloat16)
        return first, second, third

    m1, m2, m3 = split(mixed)
    lhs = jnp.concatenate([m1, m2, m1, m2, m3, m1], axis=0)
    width = math.gcd(cols, 512)

    def dot_step(c, carry):
        chunk = pl.ds(c * width, width)
        f1, f2, f3 = split(ff_ref[:, chunk])
        rhs = jnp.concatenate([f1, f1, f2, f2, f1, f3], axis=0)
        s_ref[:, chunk] = lax.dot_general(
            lhs, rhs, (((0,), (0,)), ((), ())), preferred_element_type=jnp.float32
        )
        return carry

    lax.fori_loop(0, cols // width, dot_step, 0)
    cp_ref[...] = start_ref[...] * LOG2E
    row_lse(s_ref, cp_ref, max_ref, sum_ref, out_ref)


def damped(old, log, mass):
    return 0.5 * old + 0.5 * (log - mass * LOG2E)


def col_kernel_of(parts, first):
    def kernel(*refs):
        s_ref, part_refs = refs[0], refs[1 : 1 + parts]
        old_ref, mass_ref, out_ref, log_ref, pot_ref, wide_ref, col_ref = refs[1 + parts :]
        log = lse_parts([p[...] for p in part_refs])
        old = old_ref[...] * LOG2E if first else old_ref[...]
        pot = damped(old, log, mass_ref[...])
        log_ref[...] = log
        pot_ref[...] = pot
        spread_rows(pot, wide_ref)
        col_lse(s_ref, wide_ref, col_ref)
        send_all(col_ref, out_ref)

    return kernel


def row_kernel_of(first):
    def kernel(s_ref, got_ref, old_ref, mass_ref, out_ref, log_ref, pot_ref, max_ref, sum_ref):
        log = lse_parts([got_ref[p] for p in range(got_ref.shape[0])])
        old = old_ref[...] * LOG2E if first else old_ref[...]
        log_ref[...] = log
        pot_ref[...] = damped(old, log, mass_ref[...])
        row_lse(s_ref, pot_ref, max_ref, sum_ref, out_ref)

    return kernel


def col_adjoint_pass(s_ref, wide_ref, log_ref, weight_ref, total_ref, acc_in, acc_out, out_ref):
    rows, cols = s_ref.shape
    tiles = cols // LANES
    per_step = math.gcd(rows // GROUP, 4)

    def group_step(g, carry):
        rs = [pl.ds(g * (GROUP * per_step) + q * GROUP, GROUP) for q in range(per_step)]
        shifts = [wide_ref[r, :] for r in rs]
        totals = [None] * per_step
        for k in range(tiles):
            log = log_ref[k : k + 1, :]
            weight = weight_ref[k : k + 1, :]
            for q in range(per_step):
                value = jnp.exp2(s_ref[rs[q], lane(k)] - shifts[q] - log) * weight
                totals[q] = value if totals[q] is None else totals[q] + value
                kept = value if acc_in is None else acc_in[rs[q], lane(k)] + value
                acc_out[rs[q], lane(k)] = kept
        for q in range(per_step):
            total_ref[rs[q], :] = totals[q]
        return carry

    lax.fori_loop(0, rows // (GROUP * per_step), group_step, 0)
    for block in range(rows // LANES):
        part = total_ref[pl.ds(block * LANES, LANES), :].T
        out_ref[block : block + 1, :] = jnp.sum(part, axis=0, keepdims=True)


def last_col_adjoint_kernel(s_ref, got_ref, cot_ref, pot_ref, acc_ref, out_ref, half_ref, wide_ref, total_ref, log_ref):
    log_ref[...] = lse_parts([got_ref[p] for p in range(got_ref.shape[0])])
    half_ref[...] = 0.5 * cot_ref[...]
    spread_rows(pot_ref[...], wide_ref)
    col_adjoint_pass(s_ref, wide_ref, log_ref, half_ref, total_ref, None, acc_ref, out_ref)


def col_adjoint_kernel(s_ref, acc_in, got_ref, half_in, pot_ref, log_ref, acc_ref, out_ref, half_ref, wide_ref, total_ref):
    summed = tree([got_ref[p] for p in range(got_ref.shape[0])], jnp.add)
    half_ref[...] = 0.5 * (half_in[...] - summed)
    spread_rows(pot_ref[...], wide_ref)
    col_adjoint_pass(s_ref, wide_ref, log_ref, half_ref, total_ref, acc_in, acc_ref, out_ref)


def row_adjoint_pass(s_ref, pot_ref, log_wide, weight_wide, acc_in, acc_out, col_ref):
    rows, cols = s_ref.shape
    width, chunks = col_blocking(cols)
    per_step = math.gcd(rows // GROUP, 4)

    def chunk_step(c, carry):
        pots = [
            jnp.broadcast_to(pot_ref[pl.ds(c * width + k, 1), :], (GROUP, LANES))
            for k in range(width)
        ]

        def row_step(step, totals):
            for q in range(per_step):
                r = pl.ds(step * (GROUP * per_step) + q * GROUP, GROUP)
                log = log_wide[r, :]
                weight = weight_wide[r, :]
                fresh = []
                for k in range(width):
                    at = pl.ds(c * (width * LANES) + k * LANES, LANES)
                    value = jnp.exp2(s_ref[r, at] - pots[k] - log) * weight
                    acc_out[r, at] = acc_in[r, at] + value
                    fresh.append(totals[k] + value)
                totals = tuple(fresh)
            return totals

        zero = jnp.zeros((GROUP, LANES), jnp.float32)
        totals = lax.fori_loop(0, rows // (GROUP * per_step), row_step, (zero,) * width)
        for k in range(width):
            col_ref[pl.ds(c * width + k, 1), :] = jnp.sum(totals[k], axis=0, keepdims=True)
        return carry

    lax.fori_loop(0, chunks, chunk_step, 0)


def row_adjoint_kernel_of(parts, last):
    def kernel(*refs):
        s_ref, acc_in = refs[:2]
        part_refs = refs[2 : 2 + parts]
        rest = refs[2 + parts :]
        half_in, pot_ref, log_ref = rest[:3]
        rest = rest[3:]
        if last:
            fw_ref, ff_ref, out_ref, half_ref, acc_ref, log_wide, weight_wide, col_ref, pot_scaled = rest
            pot_scaled[...] = pot_ref[...] * LOG2E
            pot_ref = pot_scaled
        else:
            acc_ref, out_ref, half_ref, log_wide, weight_wide, col_ref = rest
        summed = tree([p[...] for p in part_refs], jnp.add)
        half = 0.5 * (half_in[...] - summed)
        half_ref[...] = half
        spread_rows(log_ref[...], log_wide)
        spread_rows(half, weight_wide)
        row_adjoint_pass(s_ref, pot_ref, log_wide, weight_wide, acc_in, acc_ref, col_ref)
        if not last:
            send_all(col_ref, out_ref)
            return
        grad = contract(acc_ref, fw_ref, ff_ref)
        col_rows = col_ref.shape[0]
        value = col_ref[...]
        for peer in range(out_ref.shape[0]):
            out_ref[peer, :col_rows, :] = value
            out_ref[peer, col_rows:, :] = grad

    return kernel


def contract(acc_ref, fw_ref, ff_ref):
    rows, cols = acc_ref.shape
    rank = ff_ref.shape[0]
    width = math.gcd(cols, 512)

    def halves(value):
        first = value.astype(jnp.bfloat16)
        return first, (value - first.astype(jnp.float32)).astype(jnp.bfloat16)

    def dot_step(c, grad):
        chunk = pl.ds(c * width, width)
        f1, f2 = halves(ff_ref[:, chunk])
        rhs = jnp.concatenate([f1, f2], axis=0)
        a1, a2 = halves(acc_ref[:, chunk])
        dims = (((1,), (1,)), ((), ()))
        grad = grad + lax.dot_general(a1, rhs, dims, preferred_element_type=jnp.float32)
        return grad + lax.dot_general(a2, rhs, dims, preferred_element_type=jnp.float32)

    grad = lax.fori_loop(0, cols // width, dot_step, jnp.zeros((rows, 2 * rank), jnp.float32))
    grad = grad + pltpu.roll(grad, rank, 1)
    both = lax.dot_general(
        fw_ref[...], grad, (((0,), (0,)), ((), ())), precision=HIGHEST,
        preferred_element_type=jnp.float32,
    )
    half = rank // 2
    lanes = lax.broadcasted_iota(jnp.int32, (half, 2 * rank), 1)
    return jnp.where(lanes < rank, both[:half], both[half:])


def peers_of(part, axis):
    size = lax.axis_size(axis)
    if size & (size - 1):
        gathered = lax.all_gather(part, axis)
        return [gathered[i] for i in range(size)]
    return [part] + [
        lax.ppermute(part, axis, [(i, i ^ d) for i in range(size)]) for d in range(1, size)
    ]


def exchange_cols(block):
    return lax.all_to_all(block, "wrk", 0, 0, tiled=True)


def body(feat_wrk, feat_firm, surplus, row_start, col_start, row_mass, col_mass, row_cot, col_cot):
    rows, rank = feat_wrk.shape
    cols = feat_firm.shape[1]
    wrk, firm = lax.axis_size("wrk"), lax.axis_size("firm")
    row_dims = (rows // LANES, LANES)
    col_dims = (cols // LANES, LANES)
    row_start, row_mass, row_cot = (a.reshape(row_dims) for a in (row_start, row_mass, row_cot))
    col_start, col_mass, col_cot = (a.reshape(col_dims) for a in (col_start, col_mass, col_cot))
    wide = pltpu.VMEM((rows, LANES), jnp.float32)
    col_vec = pltpu.VMEM(col_dims, jnp.float32)
    row_out, col_out = shape_of(*row_dims), shape_of(*col_dims)
    send_out = shape_of(wrk, *col_dims)
    acc_out = shape_of(rows, cols)

    scores, part = call(
        first_row_kernel, "row_first", (acc_out, row_out),
        (feat_wrk, feat_firm, surplus, col_start),
        (col_vec, pltpu.VMEM((LANES, LANES), jnp.float32), wide, wide),
    )
    row_pots, col_pots, row_logs, col_logs = [row_start], [col_start], [], []
    for t in range(ITERS):
        parts = peers_of(part, "firm")
        block, log, pot = call(
            col_kernel_of(len(parts), t == 0), f"col_{t}", (send_out, row_out, row_out),
            (scores, *parts, row_pots[-1], row_mass), (wide, col_vec),
        )
        row_logs.append(log)
        row_pots.append(pot)
        got = exchange_cols(block)
        if t == ITERS - 1:
            break
        part, log, pot = call(
            row_kernel_of(t == 0), f"row_{t + 1}", (row_out, col_out, col_out),
            (scores, got, col_pots[-1], col_mass), (wide, wide),
        )
        col_logs.append(log)
        col_pots.append(pot)

    acc, part, col_half = call(
        last_col_adjoint_kernel, f"col_adj_{ITERS - 1}", (acc_out, row_out, col_out),
        (scores, got, col_cot, row_pots[ITERS]), (wide, wide, col_vec),
    )
    row_half = row_cot
    for t in reversed(range(ITERS)):
        parts = peers_of(part, "firm")
        args = (scores, acc, *parts, row_half, col_pots[t], row_logs[t])
        if t == 0:
            break
        acc, block, row_half = call(
            row_adjoint_kernel_of(len(parts), False), f"row_adj_{t}", (acc_out, send_out, row_out),
            args, (wide, wide, col_vec), {1: 0},
        )
        got = exchange_cols(block)
        acc, part, col_half = call(
            col_adjoint_kernel, f"col_adj_{t - 1}", (acc_out, row_out, col_out),
            (scores, acc, got, col_half, row_pots[t], col_logs[t - 1]), (wide, wide), {1: 0},
        )

    grad_rows = rank * rank // LANES
    block, row_half = call(
        row_adjoint_kernel_of(len(parts), True), "row_adj_0",
        (shape_of(wrk, col_dims[0] + grad_rows, LANES), row_out),
        (*args, feat_wrk, feat_firm),
        (pltpu.VMEM((rows, cols), jnp.float32), wide, wide, col_vec, col_vec),
    )
    summed = jnp.sum(exchange_cols(block), axis=0)
    col_bar = col_half - summed[: col_dims[0]]
    grad = tree(peers_of(summed[col_dims[0] :], "firm"), jnp.add)
    grad_surplus = jnp.concatenate([grad[:, :rank], grad[:, rank:]], axis=0)
    return (grad_surplus, row_half.reshape(rows), col_bar.reshape(cols))


def solution(mesh):
    return jax.shard_map(
        body,
        mesh=mesh,
        in_specs=(
            P("wrk", None),
            P(None, "firm"),
            P(),
            P("wrk"),
            P("firm"),
            P("wrk"),
            P("firm"),
            P("wrk"),
            P("firm"),
        ),
        out_specs=(P(), P("wrk"), P("firm")),
        check_vma=False,
    )
```

```python
import math

import jax
import jax.numpy as jnp
from jax import lax
from jax.experimental import pallas as pl
from jax.experimental.pallas import tpu as pltpu
from jax.sharding import PartitionSpec as P

ITERS = 3
LOG2E = 1.0 / math.log(2.0)
HIGHEST = lax.Precision.HIGHEST
LANES = 128
GROUP = 8
WHOLE = pl.BlockSpec(memory_space=pltpu.VMEM)
VMEM_LIMIT = 14 * 1024 * 1024


def tree(values, combine):
    values = list(values)
    while len(values) > 1:
        paired = [combine(values[i], values[i + 1]) for i in range(0, len(values) - 1, 2)]
        if len(values) % 2:
            paired.append(values[-1])
        values = paired
    return values[0]


def shape_of(*dims):
    return jax.ShapeDtypeStruct(dims, jnp.float32)


def call(kernel, name, outs, args, scratch=(), space=pltpu.VMEM):
    return pl.pallas_call(
        kernel,
        name=name,
        out_shape=outs,
        in_specs=[pl.BlockSpec(memory_space=space)] * len(args),
        out_specs=jax.tree.map(lambda _: WHOLE, outs),
        scratch_shapes=scratch,
        compiler_params=pltpu.CompilerParams(vmem_limit_bytes=VMEM_LIMIT),
    )(*args)


def lane(k):
    return pl.ds(k * LANES, LANES)


def lse_parts(parts):
    largest = tree(parts, jnp.maximum)
    return largest + jnp.log2(tree([jnp.exp2(p - largest) for p in parts], jnp.add))


def spread_rows(value, ref):
    for block in range(value.shape[0]):
        wide = jnp.broadcast_to(value[block : block + 1, :], (LANES, LANES))
        ref[pl.ds(block * LANES, LANES), :] = wide.T


def row_lse(s_ref, shift_ref, max_ref, sum_ref, out_ref):
    rows, cols = s_ref.shape
    tiles = cols // LANES
    last = rows // GROUP - 1

    def terms_of(g):
        r = pl.ds(g * GROUP, GROUP)
        terms = [s_ref[r, lane(k)] - shift_ref[k : k + 1, :] for k in range(tiles)]
        return tuple(terms), tree(terms, jnp.maximum)

    def group_step(g, carry):
        terms, largest = carry
        r = pl.ds(g * GROUP, GROUP)
        max_ref[r, :] = largest
        sum_ref[r, :] = tree([jnp.exp2(t - largest) for t in terms], jnp.add)
        return terms_of(jnp.minimum(g + 1, last))

    lax.fori_loop(0, rows // GROUP, group_step, terms_of(0))
    for block in range(rows // LANES):
        b = pl.ds(block * LANES, LANES)
        maxes = max_ref[b, :].T
        sums = sum_ref[b, :].T
        largest = jnp.max(maxes, axis=0, keepdims=True)
        total = jnp.sum(sums * jnp.exp2(maxes - largest), axis=0, keepdims=True)
        out_ref[block : block + 1, :] = largest + jnp.log2(total)


def col_blocking(cols):
    tiles = cols // LANES
    width = math.gcd(tiles, 8)
    return width, tiles // width


def send_all(col_ref, out_ref):
    value = col_ref[...]
    for peer in range(out_ref.shape[0]):
        out_ref[peer] = value


def col_lse(s_ref, shift_ref, col_ref):
    rows, cols = s_ref.shape
    width, chunks = col_blocking(cols)
    per_step = math.gcd(rows // GROUP, 8)
    steps = rows // (GROUP * per_step)
    low = jnp.full((GROUP, LANES), -jnp.inf, jnp.float32)
    zero = jnp.zeros((GROUP, LANES), jnp.float32)
    largest = None
    for chunk in range(chunks + 1):
        summing, taking = chunk > 0, chunk < chunks

        def step(i, carry):
            sums, maxes = carry
            for q in range(per_step):
                r = pl.ds(i * (GROUP * per_step) + q * GROUP, GROUP)
                shift = shift_ref[r, :]
                if summing:
                    terms = [s_ref[r, lane((chunk - 1) * width + k)] - shift for k in range(width)]
                    sums = tuple(s + jnp.exp2(t - m) for s, t, m in zip(sums, terms, largest))
                if taking:
                    terms = [s_ref[r, lane(chunk * width + k)] - shift for k in range(width)]
                    maxes = tuple(jnp.maximum(m, t) for m, t in zip(maxes, terms))
            return sums, maxes

        sums, maxes = lax.fori_loop(
            0, steps, step, ((zero,) * width if summing else (), (low,) * width if taking else ())
        )
        for k in range(width if summing else 0):
            most = jnp.max(largest[k], axis=0, keepdims=True)
            total = jnp.sum(sums[k] * jnp.exp2(largest[k] - most), axis=0, keepdims=True)
            at = (chunk - 1) * width + k
            col_ref[at : at + 1, :] = most + jnp.log2(total)
        largest = maxes


def first_row_kernel(*refs):
    count = 9
    sources, refs = refs[:count], refs[count:]
    s_ref, out_ref = refs[:2]
    held, (cp_ref, max_ref, sum_ref, sems) = refs[2 : 2 + count], refs[2 + count :]
    copies = [
        pltpu.make_async_copy(source, target, sems.at[i])
        for i, (source, target) in enumerate(zip(sources, held))
    ]
    for copy in copies:
        copy.start()
    fw_ref, ff_ref, sp_ref, start_ref = held[:4]
    for copy in copies[:3]:
        copy.wait()
    rank, cols = ff_ref.shape
    mixed = lax.dot_general(
        sp_ref[...], fw_ref[...], (((0,), (0,)), ((), ())), precision=HIGHEST,
        preferred_element_type=jnp.float32,
    ) * LOG2E

    def split(value):
        first = value.astype(jnp.bfloat16)
        rest = value - first.astype(jnp.float32)
        second = rest.astype(jnp.bfloat16)
        third = (rest - second.astype(jnp.float32)).astype(jnp.bfloat16)
        return first, second, third

    m1, m2, m3 = split(mixed)
    lhs = jnp.concatenate([m1, m2, m1, m2, m3, m1], axis=0)
    width = math.gcd(cols, 512)

    def dot_step(c, carry):
        chunk = pl.ds(c * width, width)
        f1, f2, f3 = split(ff_ref[:, chunk])
        rhs = jnp.concatenate([f1, f1, f2, f2, f1, f3], axis=0)
        s_ref[:, chunk] = lax.dot_general(
            lhs, rhs, (((0,), (0,)), ((), ())), preferred_element_type=jnp.float32
        )
        return carry

    lax.fori_loop(0, cols // width, dot_step, 0)
    for copy in copies[3:]:
        copy.wait()
    cp_ref[...] = start_ref[...] * LOG2E
    row_lse(s_ref, cp_ref, max_ref, sum_ref, out_ref)


def damped(old, log, mass):
    return 0.5 * old + 0.5 * (log - mass * LOG2E)


def col_kernel_of(parts, first):
    def kernel(*refs):
        s_ref, part_refs = refs[0], refs[1 : 1 + parts]
        old_ref, mass_ref, out_ref, log_ref, pot_ref, wide_ref, col_ref = refs[1 + parts :]
        log = lse_parts([p[...] for p in part_refs])
        old = old_ref[...] * LOG2E if first else old_ref[...]
        pot = damped(old, log, mass_ref[...])
        log_ref[...] = log
        pot_ref[...] = pot
        spread_rows(pot, wide_ref)
        col_lse(s_ref, wide_ref, col_ref)
        send_all(col_ref, out_ref)

    return kernel


def row_kernel_of(first):
    def kernel(s_ref, got_ref, old_ref, mass_ref, out_ref, log_ref, pot_ref, max_ref, sum_ref):
        log = lse_parts([got_ref[p] for p in range(got_ref.shape[0])])
        old = old_ref[...] * LOG2E if first else old_ref[...]
        log_ref[...] = log
        pot_ref[...] = damped(old, log, mass_ref[...])
        row_lse(s_ref, pot_ref, max_ref, sum_ref, out_ref)

    return kernel


def col_adjoint_pass(s_ref, wide_ref, log_ref, weight_ref, total_ref, acc_in, acc_out, out_ref):
    rows, cols = s_ref.shape
    tiles = cols // LANES
    per_step = math.gcd(rows // GROUP, 4)

    def group_step(g, carry):
        rs = [pl.ds(g * (GROUP * per_step) + q * GROUP, GROUP) for q in range(per_step)]
        shifts = [wide_ref[r, :] for r in rs]
        totals = [None] * per_step
        for k in range(tiles):
            log = log_ref[k : k + 1, :]
            weight = weight_ref[k : k + 1, :]
            for q in range(per_step):
                value = jnp.exp2(s_ref[rs[q], lane(k)] - shifts[q] - log) * weight
                totals[q] = value if totals[q] is None else totals[q] + value
                kept = value if acc_in is None else acc_in[rs[q], lane(k)] + value
                acc_out[rs[q], lane(k)] = kept
        for q in range(per_step):
            total_ref[rs[q], :] = totals[q]
        return carry

    lax.fori_loop(0, rows // (GROUP * per_step), group_step, 0)
    for block in range(rows // LANES):
        part = total_ref[pl.ds(block * LANES, LANES), :].T
        out_ref[block : block + 1, :] = jnp.sum(part, axis=0, keepdims=True)


def last_col_adjoint_kernel(s_ref, got_ref, cot_ref, pot_ref, acc_ref, out_ref, half_ref, wide_ref, total_ref, log_ref):
    log_ref[...] = lse_parts([got_ref[p] for p in range(got_ref.shape[0])])
    half_ref[...] = 0.5 * cot_ref[...]
    spread_rows(pot_ref[...], wide_ref)
    col_adjoint_pass(s_ref, wide_ref, log_ref, half_ref, total_ref, None, acc_ref, out_ref)


def col_adjoint_kernel(s_ref, acc_in, got_ref, half_in, pot_ref, log_ref, acc_ref, out_ref, half_ref, wide_ref, total_ref):
    summed = tree([got_ref[p] for p in range(got_ref.shape[0])], jnp.add)
    half_ref[...] = 0.5 * (half_in[...] - summed)
    spread_rows(pot_ref[...], wide_ref)
    col_adjoint_pass(s_ref, wide_ref, log_ref, half_ref, total_ref, acc_in, acc_ref, out_ref)


def row_adjoint_pass(s_ref, pot_ref, log_wide, weight_wide, acc_in, acc_out, col_ref):
    rows, cols = s_ref.shape
    width, chunks = col_blocking(cols)
    per_step = math.gcd(rows // GROUP, 4)

    for c in range(chunks):
        first = c * width
        pots = [
            jnp.broadcast_to(pot_ref[first + k : first + k + 1, :], (GROUP, LANES))
            for k in range(width)
        ]

        def row_step(step, totals):
            for q in range(per_step):
                r = pl.ds(step * (GROUP * per_step) + q * GROUP, GROUP)
                log = log_wide[r, :]
                weight = weight_wide[r, :]
                fresh = []
                for k in range(width):
                    value = jnp.exp2(s_ref[r, lane(first + k)] - pots[k] - log) * weight
                    acc_out[r, lane(first + k)] = acc_in[r, lane(first + k)] + value
                    fresh.append(totals[k] + value)
                totals = tuple(fresh)
            return totals

        zero = jnp.zeros((GROUP, LANES), jnp.float32)
        totals = lax.fori_loop(0, rows // (GROUP * per_step), row_step, (zero,) * width)
        for k in range(width):
            col_ref[first + k : first + k + 1, :] = jnp.sum(totals[k], axis=0, keepdims=True)


def row_adjoint_kernel_of(parts, last):
    def kernel(*refs):
        s_ref, acc_in = refs[:2]
        part_refs = refs[2 : 2 + parts]
        rest = refs[2 + parts :]
        half_in, pot_ref, log_ref = rest[:3]
        rest = rest[3:]
        if last:
            fw_ref, ff_ref, out_ref, half_ref, acc_ref, log_wide, weight_wide, col_ref, pot_scaled = rest
            pot_scaled[...] = pot_ref[...] * LOG2E
            pot_ref = pot_scaled
        else:
            acc_ref, out_ref, half_ref, log_wide, weight_wide, col_ref = rest
        summed = tree([p[...] for p in part_refs], jnp.add)
        half = 0.5 * (half_in[...] - summed)
        half_ref[...] = half
        spread_rows(log_ref[...], log_wide)
        spread_rows(half, weight_wide)
        row_adjoint_pass(s_ref, pot_ref, log_wide, weight_wide, acc_in, acc_ref, col_ref)
        if not last:
            send_all(col_ref, out_ref)
            return
        grad = contract(acc_ref, fw_ref, ff_ref)
        col_rows = col_ref.shape[0]
        value = col_ref[...]
        for peer in range(out_ref.shape[0]):
            out_ref[peer, :col_rows, :] = value
            out_ref[peer, col_rows:, :] = grad

    return kernel


def contract(acc_ref, fw_ref, ff_ref):
    rows, cols = acc_ref.shape
    rank = ff_ref.shape[0]
    width = math.gcd(cols, 512)

    def halves(value):
        first = value.astype(jnp.bfloat16)
        return first, (value - first.astype(jnp.float32)).astype(jnp.bfloat16)

    def dot_step(c, grad):
        chunk = pl.ds(c * width, width)
        f1, f2 = halves(ff_ref[:, chunk])
        rhs = jnp.concatenate([f1, f2], axis=0)
        a1, a2 = halves(acc_ref[:, chunk])
        dims = (((1,), (1,)), ((), ()))
        grad = grad + lax.dot_general(a1, rhs, dims, preferred_element_type=jnp.float32)
        return grad + lax.dot_general(a2, rhs, dims, preferred_element_type=jnp.float32)

    grad = lax.fori_loop(0, cols // width, dot_step, jnp.zeros((rows, 2 * rank), jnp.float32))
    grad = grad + pltpu.roll(grad, rank, 1)
    both = lax.dot_general(
        fw_ref[...], grad, (((1,), (0,)), ((), ())), precision=HIGHEST,
        preferred_element_type=jnp.float32,
    )
    half = rank // 2
    lanes = lax.broadcasted_iota(jnp.int32, (half, 2 * rank), 1)
    return jnp.where(lanes < rank, both[:half], both[half:])


def peers_of(part, axis):
    size = lax.axis_size(axis)
    if size & (size - 1):
        gathered = lax.all_gather(part, axis)
        return [gathered[i] for i in range(size)]
    return [part] + [
        lax.ppermute(part, axis, [(i, i ^ d) for i in range(size)]) for d in range(1, size)
    ]


def exchange_cols(block):
    return lax.all_to_all(block, "wrk", 0, 0, tiled=True)


def body(feat_wrk, feat_firm, surplus, row_start, col_start, row_mass, col_mass, row_cot, col_cot):
    rows, rank = feat_wrk.shape
    cols = feat_firm.shape[1]
    wrk, firm = lax.axis_size("wrk"), lax.axis_size("firm")
    row_dims = (rows // LANES, LANES)
    col_dims = (cols // LANES, LANES)
    row_start, row_mass, row_cot = (a.reshape(row_dims) for a in (row_start, row_mass, row_cot))
    col_start, col_mass, col_cot = (a.reshape(col_dims) for a in (col_start, col_mass, col_cot))
    wide = pltpu.VMEM((rows, LANES), jnp.float32)
    col_vec = pltpu.VMEM(col_dims, jnp.float32)
    row_out, col_out = shape_of(*row_dims), shape_of(*col_dims)
    send_out = shape_of(wrk, *col_dims)
    acc_out = shape_of(rows, cols)

    inputs = (feat_wrk.T, feat_firm, surplus, col_start, row_start, row_mass, col_mass, row_cot, col_cot)
    inputs = tuple(pltpu.with_memory_space_constraint(a, pltpu.HBM) for a in inputs)
    scores, part, *held = call(
        first_row_kernel, "row_first", (acc_out, row_out, *(shape_of(*a.shape) for a in inputs)), inputs,
        (col_vec, wide, wide, pltpu.SemaphoreType.DMA((len(inputs),))), pltpu.HBM,
    )
    feat_wrk, feat_firm, surplus, col_start, row_start, row_mass, col_mass, row_cot, col_cot = held
    row_pots, col_pots, row_logs, col_logs = [row_start], [col_start], [], []
    for t in range(ITERS):
        parts = peers_of(part, "firm")
        block, log, pot = call(
            col_kernel_of(len(parts), t == 0), f"col_{t}", (send_out, row_out, row_out),
            (scores, *parts, row_pots[-1], row_mass), (wide, col_vec),
        )
        row_logs.append(log)
        row_pots.append(pot)
        got = exchange_cols(block)
        if t == ITERS - 1:
            break
        part, log, pot = call(
            row_kernel_of(t == 0), f"row_{t + 1}", (row_out, col_out, col_out),
            (scores, got, col_pots[-1], col_mass), (wide, wide),
        )
        col_logs.append(log)
        col_pots.append(pot)

    acc, part, col_half = call(
        last_col_adjoint_kernel, f"col_adj_{ITERS - 1}", (acc_out, row_out, col_out),
        (scores, got, col_cot, row_pots[ITERS]), (wide, wide, col_vec),
    )
    row_half = row_cot
    for t in reversed(range(ITERS)):
        parts = peers_of(part, "firm")
        args = (scores, acc, *parts, row_half, col_pots[t], row_logs[t])
        if t == 0:
            break
        acc, block, row_half = call(
            row_adjoint_kernel_of(len(parts), False), f"row_adj_{t}", (acc_out, send_out, row_out),
            args, (wide, wide, col_vec),
        )
        got = exchange_cols(block)
        acc, part, col_half = call(
            col_adjoint_kernel, f"col_adj_{t - 1}", (acc_out, row_out, col_out),
            (scores, acc, got, col_half, row_pots[t], col_logs[t - 1]), (wide, wide),
        )

    grad_rows = rank * rank // LANES
    block, row_half = call(
        row_adjoint_kernel_of(len(parts), True), "row_adj_0",
        (shape_of(wrk, col_dims[0] + grad_rows, LANES), row_out),
        (*args, feat_wrk, feat_firm),
        (pltpu.VMEM((rows, cols), jnp.float32), wide, wide, col_vec, col_vec),
    )
    summed = jnp.sum(exchange_cols(block), axis=0)
    col_bar = col_half - summed[: col_dims[0]]
    grad = tree(peers_of(summed[col_dims[0] :], "firm"), jnp.add)
    grad_surplus = jnp.concatenate([grad[:, :rank], grad[:, rank:]], axis=0)
    return (grad_surplus, row_half.reshape(rows), col_bar.reshape(cols))


def solution(mesh):
    return jax.shard_map(
        body,
        mesh=mesh,
        in_specs=(
            P("wrk", None),
            P(None, "firm"),
            P(),
            P("wrk"),
            P("firm"),
            P("wrk"),
            P("firm"),
            P("wrk"),
            P("firm"),
        ),
        out_specs=(P(), P("wrk"), P("firm")),
        check_vma=False,
    )
```

```python
import math

import jax
import jax.numpy as jnp
from jax import lax
from jax.experimental import pallas as pl
from jax.experimental.pallas import tpu as pltpu
from jax.sharding import PartitionSpec as P

ITERS = 3
LOG2E = 1.0 / math.log(2.0)
HIGHEST = lax.Precision.HIGHEST
LANES = 128
GROUP = 8
WHOLE = pl.BlockSpec(memory_space=pltpu.VMEM)
VMEM_LIMIT = 14 * 1024 * 1024


def tree(values, combine):
    values = list(values)
    while len(values) > 1:
        paired = [combine(values[i], values[i + 1]) for i in range(0, len(values) - 1, 2)]
        if len(values) % 2:
            paired.append(values[-1])
        values = paired
    return values[0]


def shape_of(*dims):
    return jax.ShapeDtypeStruct(dims, jnp.float32)


def call(kernel, name, outs, args, scratch=(), space=pltpu.VMEM):
    return pl.pallas_call(
        kernel,
        name=name,
        out_shape=outs,
        in_specs=[pl.BlockSpec(memory_space=space)] * len(args),
        out_specs=jax.tree.map(lambda _: WHOLE, outs),
        scratch_shapes=scratch,
        compiler_params=pltpu.CompilerParams(vmem_limit_bytes=VMEM_LIMIT),
    )(*args)


def loop(count, body, init):
    for i in range(count):
        init = body(i, init)
    return init


def lane(k):
    return pl.ds(k * LANES, LANES)


def lse_parts(parts):
    largest = tree(parts, jnp.maximum)
    return largest + jnp.log2(tree([jnp.exp2(p - largest) for p in parts], jnp.add))


def spread_rows(value, ref):
    for block in range(value.shape[0]):
        wide = jnp.broadcast_to(value[block : block + 1, :], (LANES, LANES))
        ref[pl.ds(block * LANES, LANES), :] = wide.T


def row_lse_chunk(s_ref, shift_ref, max_ref, sum_ref, first, width, groups, later):
    shifts = [wide_lane(shift_ref, first + k) for k in range(width)]
    for g in groups:
        r = pl.ds(g * GROUP, GROUP)
        terms = [s_ref[r, lane(first + k)] - shifts[k] for k in range(width)]
        largest = tree(terms, jnp.maximum)
        if later:
            before = max_ref[r, :]
            largest = jnp.maximum(largest, before)
        total = tree([jnp.exp2(t - largest) for t in terms], jnp.add)
        if later:
            total = total + sum_ref[r, :] * jnp.exp2(before - largest)
        max_ref[r, :] = largest
        sum_ref[r, :] = total


def row_lse_end(max_ref, sum_ref, out_ref):
    for block in range(max_ref.shape[0] // LANES):
        b = pl.ds(block * LANES, LANES)
        maxes = max_ref[b, :].T
        sums = sum_ref[b, :].T
        largest = jnp.max(maxes, axis=0, keepdims=True)
        total = jnp.sum(sums * jnp.exp2(maxes - largest), axis=0, keepdims=True)
        out_ref[block : block + 1, :] = largest + jnp.log2(total)


def row_lse(s_ref, shift_ref, max_ref, sum_ref, out_ref):
    rows, cols = s_ref.shape
    width, chunks = col_blocking(cols, 8)
    per_step = math.gcd(rows // GROUP, 8)
    for chunk in range(chunks):

        def step(i, carry):
            groups = [i * per_step + q for q in range(per_step)]
            row_lse_chunk(s_ref, shift_ref, max_ref, sum_ref, chunk * width, width, groups, chunk > 0)
            return carry

        loop(rows // (GROUP * per_step), step, 0)
    row_lse_end(max_ref, sum_ref, out_ref)


def col_blocking(cols, most):
    tiles = cols // LANES
    width = math.gcd(tiles, most)
    return width, tiles // width


def wide_lane(ref, k):
    return jnp.broadcast_to(ref[k : k + 1, :], (GROUP, LANES))


def send_all(col_ref, out_ref):
    value = col_ref[...]
    for peer in range(out_ref.shape[0]):
        out_ref[peer] = value


def col_lse(s_ref, shift_ref, col_ref):
    rows, cols = s_ref.shape
    width, chunks = col_blocking(cols, 8)
    per_step = math.gcd(rows // GROUP, 8)
    steps = rows // (GROUP * per_step)
    low = jnp.full((GROUP, LANES), -jnp.inf, jnp.float32)
    zero = jnp.zeros((GROUP, LANES), jnp.float32)
    largest = None
    for chunk in range(chunks + 1):
        summing, taking = chunk > 0, chunk < chunks

        def step(i, carry):
            sums, maxes = carry
            for q in range(per_step):
                r = pl.ds(i * (GROUP * per_step) + q * GROUP, GROUP)
                shift = shift_ref[r, :]
                if summing:
                    terms = [s_ref[r, lane((chunk - 1) * width + k)] - shift for k in range(width)]
                    sums = tuple(s + jnp.exp2(t - m) for s, t, m in zip(sums, terms, largest))
                if taking:
                    terms = [s_ref[r, lane(chunk * width + k)] - shift for k in range(width)]
                    maxes = tuple(jnp.maximum(m, t) for m, t in zip(maxes, terms))
            return sums, maxes

        sums, maxes = loop(
            steps, step, ((zero,) * width if summing else (), (low,) * width if taking else ())
        )
        for k in range(width if summing else 0):
            most = jnp.max(largest[k], axis=0, keepdims=True)
            total = jnp.sum(sums[k] * jnp.exp2(largest[k] - most), axis=0, keepdims=True)
            at = (chunk - 1) * width + k
            col_ref[at : at + 1, :] = most + jnp.log2(total)
        largest = maxes


def first_row_kernel(*refs):
    count = 9
    sources, refs = refs[:count], refs[count:]
    s_ref, out_ref = refs[:2]
    held, (lhs_ref, cp_ref, max_ref, sum_ref, sems) = refs[2 : 2 + count], refs[2 + count :]
    copies = [
        pltpu.make_async_copy(source, target, sems.at[i])
        for i, (source, target) in enumerate(zip(sources, held))
    ]
    for copy in copies:
        copy.start()
    fw_ref, ff_ref, sp_ref, start_ref = held[:4]
    copies[0].wait()
    copies[2].wait()
    rank, cols = ff_ref.shape
    mixed = lax.dot_general(
        sp_ref[...], fw_ref[...], (((0,), (0,)), ((), ())), precision=HIGHEST,
        preferred_element_type=jnp.float32,
    ) * LOG2E

    def split(value):
        first = value.astype(jnp.bfloat16)
        rest = value - first.astype(jnp.float32)
        second = rest.astype(jnp.bfloat16)
        third = (rest - second.astype(jnp.float32)).astype(jnp.bfloat16)
        return first, second, third

    m1, m2, m3 = split(mixed)
    stacked = jnp.concatenate([m.astype(jnp.float32) for m in (m1, m2, m1, m2, m3, m1)], axis=0)
    lhs_ref[...] = stacked.T.astype(jnp.bfloat16)
    copies[1].wait()
    width = math.gcd(cols, 512)
    copies[3].wait()
    cp_ref[...] = start_ref[...] * LOG2E

    def dot_step(c):
        chunk = pl.ds(c * width, width)
        f1, f2, f3 = split(ff_ref[:, chunk])
        rhs = jnp.concatenate([f1, f1, f2, f2, f1, f3], axis=0)
        s_ref[:, chunk] = lax.dot_general(
            lhs_ref[...], rhs, (((1,), (0,)), ((), ())), preferred_element_type=jnp.float32
        )

    tiles = width // LANES
    rows = s_ref.shape[0]
    for c in range(cols // width + 1):
        if c < cols // width:
            dot_step(c)
        if c:
            row_lse_chunk(s_ref, cp_ref, max_ref, sum_ref, (c - 1) * tiles, tiles, range(rows // GROUP), c > 1)
    row_lse_end(max_ref, sum_ref, out_ref)
    for copy in copies[4:]:
        copy.wait()


def damped(old, log, mass):
    return 0.5 * old + 0.5 * (log - mass * LOG2E)


def col_kernel_of(parts, first):
    def kernel(*refs):
        s_ref, part_refs = refs[0], refs[1 : 1 + parts]
        old_ref, mass_ref, out_ref, log_ref, pot_ref, wide_ref, col_ref = refs[1 + parts :]
        log = lse_parts([p[...] for p in part_refs])
        old = old_ref[...] * LOG2E if first else old_ref[...]
        pot = damped(old, log, mass_ref[...])
        log_ref[...] = log
        pot_ref[...] = pot
        spread_rows(pot, wide_ref)
        col_lse(s_ref, wide_ref, col_ref)
        send_all(col_ref, out_ref)

    return kernel


def row_kernel_of(first):
    def kernel(s_ref, got_ref, old_ref, mass_ref, out_ref, log_ref, pot_ref, max_ref, sum_ref):
        log = lse_parts([got_ref[p] for p in range(got_ref.shape[0])])
        old = old_ref[...] * LOG2E if first else old_ref[...]
        log_ref[...] = log
        pot_ref[...] = damped(old, log, mass_ref[...])
        row_lse(s_ref, pot_ref, max_ref, sum_ref, out_ref)

    return kernel


def col_adjoint_pass(s_ref, wide_ref, log_ref, weight_ref, total_ref, acc_in, acc_out, out_ref):
    rows, cols = s_ref.shape
    width, chunks = col_blocking(cols, 8)
    for c in range(chunks):
        first = c * width
        logs = [wide_lane(log_ref, first + k) for k in range(width)]
        weights = [wide_lane(weight_ref, first + k) for k in range(width)]
        for g in range(rows // GROUP):
            r = pl.ds(g * GROUP, GROUP)
            shift = wide_ref[r, :]
            values = []
            for k in range(width):
                at = lane(first + k)
                value = jnp.exp2(s_ref[r, at] - shift - logs[k]) * weights[k]
                acc_out[r, at] = value if acc_in is None else acc_in[r, at] + value
                values.append(value)
            total = tree(values, jnp.add)
            total_ref[r, :] = total_ref[r, :] + total if c else total
    for block in range(rows // LANES):
        part = total_ref[pl.ds(block * LANES, LANES), :].T
        out_ref[block : block + 1, :] = jnp.sum(part, axis=0, keepdims=True)


def last_col_adjoint_kernel(s_ref, got_ref, cot_ref, pot_ref, acc_ref, out_ref, half_ref, wide_ref, total_ref, log_ref):
    log_ref[...] = lse_parts([got_ref[p] for p in range(got_ref.shape[0])])
    half_ref[...] = 0.5 * cot_ref[...]
    spread_rows(pot_ref[...], wide_ref)
    col_adjoint_pass(s_ref, wide_ref, log_ref, half_ref, total_ref, None, acc_ref, out_ref)


def col_adjoint_kernel(s_ref, acc_in, got_ref, half_in, pot_ref, log_ref, acc_ref, out_ref, half_ref, wide_ref, total_ref):
    summed = tree([got_ref[p] for p in range(got_ref.shape[0])], jnp.add)
    half_ref[...] = 0.5 * (half_in[...] - summed)
    spread_rows(pot_ref[...], wide_ref)
    col_adjoint_pass(s_ref, wide_ref, log_ref, half_ref, total_ref, acc_in, acc_ref, out_ref)


def row_adjoint_pass(s_ref, pot_ref, log_wide, weight_wide, acc_in, acc_out, col_ref):
    rows, cols = s_ref.shape
    width, chunks = col_blocking(cols, 8)
    per_step = math.gcd(rows // GROUP, 8)

    for c in range(chunks):
        first = c * width
        pots = [wide_lane(pot_ref, first + k) for k in range(width)]

        def row_step(step, totals):
            for q in range(per_step):
                r = pl.ds(step * (GROUP * per_step) + q * GROUP, GROUP)
                log = log_wide[r, :]
                weight = weight_wide[r, :]
                fresh = []
                for k in range(width):
                    value = jnp.exp2(s_ref[r, lane(first + k)] - pots[k] - log) * weight
                    acc_out[r, lane(first + k)] = acc_in[r, lane(first + k)] + value
                    fresh.append(totals[k] + value)
                totals = tuple(fresh)
            return totals

        zero = jnp.zeros((GROUP, LANES), jnp.float32)
        totals = loop(rows // (GROUP * per_step), row_step, (zero,) * width)
        for k in range(width):
            col_ref[first + k : first + k + 1, :] = jnp.sum(totals[k], axis=0, keepdims=True)


def row_adjoint_kernel_of(parts, last):
    def kernel(*refs):
        s_ref, acc_in = refs[:2]
        part_refs = refs[2 : 2 + parts]
        rest = refs[2 + parts :]
        half_in, pot_ref, log_ref = rest[:3]
        rest = rest[3:]
        if last:
            fw_ref, ff_ref, out_ref, half_ref, acc_ref, log_wide, weight_wide, col_ref, pot_scaled = rest
            pot_scaled[...] = pot_ref[...] * LOG2E
            pot_ref = pot_scaled
        else:
            acc_ref, out_ref, half_ref, log_wide, weight_wide, col_ref = rest
        summed = tree([p[...] for p in part_refs], jnp.add)
        half = 0.5 * (half_in[...] - summed)
        half_ref[...] = half
        spread_rows(log_ref[...], log_wide)
        spread_rows(half, weight_wide)
        row_adjoint_pass(s_ref, pot_ref, log_wide, weight_wide, acc_in, acc_ref, col_ref)
        if not last:
            send_all(col_ref, out_ref)
            return
        grad = contract(acc_ref, fw_ref, ff_ref)
        col_rows = col_ref.shape[0]
        value = col_ref[...]
        for peer in range(out_ref.shape[0]):
            out_ref[peer, :col_rows, :] = value
            out_ref[peer, col_rows:, :] = grad

    return kernel


def contract(acc_ref, fw_ref, ff_ref):
    rows, cols = acc_ref.shape
    rank = ff_ref.shape[0]
    width = math.gcd(cols, 512)

    def halves(value):
        first = value.astype(jnp.bfloat16)
        return first, (value - first.astype(jnp.float32)).astype(jnp.bfloat16)

    def dot_step(c, grad):
        chunk = pl.ds(c * width, width)
        f1, f2 = halves(ff_ref[:, chunk])
        rhs = jnp.concatenate([f1, f2], axis=0)
        lhs = jnp.concatenate(halves(acc_ref[:, chunk]), axis=1)
        return grad + lax.dot_general(
            lhs, jnp.concatenate([rhs, rhs], axis=1), (((1,), (1,)), ((), ())),
            preferred_element_type=jnp.float32,
        )

    grad = lax.fori_loop(0, cols // width, dot_step, jnp.zeros((rows, 2 * rank), jnp.float32))
    grad = grad + pltpu.roll(grad, rank, 1)
    both = lax.dot_general(
        fw_ref[...], grad, (((1,), (0,)), ((), ())), precision=HIGHEST,
        preferred_element_type=jnp.float32,
    )
    half = rank // 2
    lanes = lax.broadcasted_iota(jnp.int32, (half, 2 * rank), 1)
    return jnp.where(lanes < rank, both[:half], both[half:])


def unfold_kernel(*refs):
    grad = tree([ref[...] for ref in refs[:-1]], jnp.add)
    half, lanes = grad.shape
    rank = lanes // 2
    refs[-1][:half, :] = grad[:, :rank]
    refs[-1][half:, :] = pltpu.roll(grad, rank, 1)[:, :rank]


def peers_of(part, axis):
    size = lax.axis_size(axis)
    if size & (size - 1):
        gathered = lax.all_gather(part, axis)
        return [gathered[i] for i in range(size)]
    return [part] + [
        lax.ppermute(part, axis, [(i, i ^ d) for i in range(size)]) for d in range(1, size)
    ]


def exchange_cols(block):
    return lax.all_to_all(block, "wrk", 0, 0, tiled=True)


def body(feat_wrk, feat_firm, surplus, row_start, col_start, row_mass, col_mass, row_cot, col_cot):
    rows, rank = feat_wrk.shape
    cols = feat_firm.shape[1]
    wrk, firm = lax.axis_size("wrk"), lax.axis_size("firm")
    row_dims = (rows // LANES, LANES)
    col_dims = (cols // LANES, LANES)
    row_start, row_mass, row_cot = (a.reshape(row_dims) for a in (row_start, row_mass, row_cot))
    col_start, col_mass, col_cot = (a.reshape(col_dims) for a in (col_start, col_mass, col_cot))
    wide = pltpu.VMEM((rows, LANES), jnp.float32)
    col_vec = pltpu.VMEM(col_dims, jnp.float32)
    row_out, col_out = shape_of(*row_dims), shape_of(*col_dims)
    send_out = shape_of(wrk, *col_dims)
    acc_out = shape_of(rows, cols)

    inputs = (feat_wrk.T, feat_firm, surplus, col_start, row_start, row_mass, col_mass, row_cot, col_cot)
    inputs = tuple(pltpu.with_memory_space_constraint(a, pltpu.HBM) for a in inputs)
    scores, part, *held = call(
        first_row_kernel, "row_first", (acc_out, row_out, *(shape_of(*a.shape) for a in inputs)), inputs,
        (
            pltpu.VMEM((rows, 6 * rank), jnp.bfloat16), col_vec, wide, wide,
            pltpu.SemaphoreType.DMA((len(inputs),)),
        ),
        pltpu.HBM,
    )
    feat_wrk, feat_firm, surplus, col_start, row_start, row_mass, col_mass, row_cot, col_cot = held
    row_pots, col_pots, row_logs, col_logs = [row_start], [col_start], [], []
    for t in range(ITERS):
        parts = peers_of(part, "firm")
        block, log, pot = call(
            col_kernel_of(len(parts), t == 0), f"col_{t}", (send_out, row_out, row_out),
            (scores, *parts, row_pots[-1], row_mass), (wide, col_vec),
        )
        row_logs.append(log)
        row_pots.append(pot)
        got = exchange_cols(block)
        if t == ITERS - 1:
            break
        part, log, pot = call(
            row_kernel_of(t == 0), f"row_{t + 1}", (row_out, col_out, col_out),
            (scores, got, col_pots[-1], col_mass), (wide, wide),
        )
        col_logs.append(log)
        col_pots.append(pot)

    acc, part, col_half = call(
        last_col_adjoint_kernel, f"col_adj_{ITERS - 1}", (acc_out, row_out, col_out),
        (scores, got, col_cot, row_pots[ITERS]), (wide, wide, col_vec),
    )
    row_half = row_cot
    for t in reversed(range(ITERS)):
        parts = peers_of(part, "firm")
        args = (scores, acc, *parts, row_half, col_pots[t], row_logs[t])
        if t == 0:
            break
        acc, block, row_half = call(
            row_adjoint_kernel_of(len(parts), False), f"row_adj_{t}", (acc_out, send_out, row_out),
            args, (wide, wide, col_vec),
        )
        got = exchange_cols(block)
        acc, part, col_half = call(
            col_adjoint_kernel, f"col_adj_{t - 1}", (acc_out, row_out, col_out),
            (scores, acc, got, col_half, row_pots[t], col_logs[t - 1]), (wide, wide),
        )

    grad_rows = rank * rank // LANES
    block, row_half = call(
        row_adjoint_kernel_of(len(parts), True), "row_adj_0",
        (shape_of(wrk, col_dims[0] + grad_rows, LANES), row_out),
        (*args, feat_wrk, feat_firm),
        (pltpu.VMEM((rows, cols), jnp.float32), wide, wide, col_vec, col_vec),
    )
    summed = jnp.sum(exchange_cols(block), axis=0)
    col_bar = (col_half - summed[: col_dims[0]]).reshape(cols)
    summed = summed[col_dims[0] :]
    grad_surplus = call(
        unfold_kernel, "unfold", shape_of(rank, rank), peers_of(summed, "firm")
    )
    return (grad_surplus, row_half.reshape(rows), col_bar)


def solution(mesh):
    return jax.shard_map(
        body,
        mesh=mesh,
        in_specs=(
            P("wrk", None),
            P(None, "firm"),
            P(),
            P("wrk"),
            P("firm"),
            P("wrk"),
            P("firm"),
            P("wrk"),
            P("firm"),
        ),
        out_specs=(P(), P("wrk"), P("firm")),
        check_vma=False,
    )
```

```python
import math

import jax
import jax.numpy as jnp
from jax import lax
from jax.experimental import pallas as pl
from jax.experimental.pallas import tpu as pltpu
from jax.sharding import PartitionSpec as P

ITERS = 3
LOG2E = 1.0 / math.log(2.0)
HIGHEST = lax.Precision.HIGHEST
LANES = 128
GROUP = 8
WHOLE = pl.BlockSpec(memory_space=pltpu.VMEM)
VMEM_LIMIT = 14 * 1024 * 1024


def tree(values, combine):
    values = list(values)
    while len(values) > 1:
        paired = [combine(values[i], values[i + 1]) for i in range(0, len(values) - 1, 2)]
        if len(values) % 2:
            paired.append(values[-1])
        values = paired
    return values[0]


def shape_of(*dims):
    return jax.ShapeDtypeStruct(dims, jnp.float32)


def call(kernel, name, outs, args, scratch=(), space=pltpu.VMEM):
    return pl.pallas_call(
        kernel,
        name=name,
        out_shape=outs,
        in_specs=[pl.BlockSpec(memory_space=space)] * len(args),
        out_specs=jax.tree.map(lambda _: WHOLE, outs),
        scratch_shapes=scratch,
        compiler_params=pltpu.CompilerParams(vmem_limit_bytes=VMEM_LIMIT),
    )(*args)


def lane(k):
    return pl.ds(k * LANES, LANES)


def lse_parts(parts):
    largest = tree(parts, jnp.maximum)
    return largest + jnp.log2(tree([jnp.exp2(p - largest) for p in parts], jnp.add))


def spread_rows(value, ref):
    for block in range(value.shape[0]):
        wide = jnp.broadcast_to(value[block : block + 1, :], (LANES, LANES))
        ref[pl.ds(block * LANES, LANES), :] = wide.T


def row_lse_chunk(s_ref, shift_ref, max_ref, sum_ref, first, width, groups, later):
    shifts = [wide_lane(shift_ref, first + k) for k in range(width)]
    for g in groups:
        r = pl.ds(g * GROUP, GROUP)
        terms = [s_ref[r, lane(first + k)] - shifts[k] for k in range(width)]
        largest = tree(terms, jnp.maximum)
        if later:
            before = max_ref[r, :]
            largest = jnp.maximum(largest, before)
        total = tree([jnp.exp2(t - largest) for t in terms], jnp.add)
        if later:
            total = total + sum_ref[r, :] * jnp.exp2(before - largest)
        max_ref[r, :] = largest
        sum_ref[r, :] = total


def row_lse_end(max_ref, sum_ref, out_ref):
    for block in range(max_ref.shape[0] // LANES):
        b = pl.ds(block * LANES, LANES)
        maxes = max_ref[b, :].T
        sums = sum_ref[b, :].T
        largest = jnp.max(maxes, axis=0, keepdims=True)
        total = jnp.sum(sums * jnp.exp2(maxes - largest), axis=0, keepdims=True)
        out_ref[block : block + 1, :] = largest + jnp.log2(total)


def row_lse(s_ref, shift_ref, max_ref, sum_ref, out_ref):
    rows, cols = s_ref.shape
    width, chunks = col_blocking(cols, 8)
    per_step = math.gcd(rows // GROUP, 8)
    for chunk in range(chunks):

        def step(i, carry):
            groups = [i * per_step + q for q in range(per_step)]
            row_lse_chunk(s_ref, shift_ref, max_ref, sum_ref, chunk * width, width, groups, chunk > 0)
            return carry

        lax.fori_loop(0, rows // (GROUP * per_step), step, 0)
    row_lse_end(max_ref, sum_ref, out_ref)


def col_blocking(cols, most):
    tiles = cols // LANES
    width = math.gcd(tiles, most)
    return width, tiles // width


def wide_lane(ref, k):
    return jnp.broadcast_to(ref[k : k + 1, :], (GROUP, LANES))


def send_all(col_ref, out_ref):
    value = col_ref[...]
    for peer in range(out_ref.shape[0]):
        out_ref[peer] = value


def col_lse(s_ref, shift_ref, col_ref):
    rows, cols = s_ref.shape
    width, chunks = col_blocking(cols, 8)
    per_step = math.gcd(rows // GROUP, 8)
    steps = rows // (GROUP * per_step)
    low = jnp.full((GROUP, LANES), -jnp.inf, jnp.float32)
    zero = jnp.zeros((GROUP, LANES), jnp.float32)
    largest = None
    for chunk in range(chunks + 1):
        summing, taking = chunk > 0, chunk < chunks

        def step(i, carry):
            sums, maxes = carry
            for q in range(per_step):
                r = pl.ds(i * (GROUP * per_step) + q * GROUP, GROUP)
                shift = shift_ref[r, :]
                if summing:
                    terms = [s_ref[r, lane((chunk - 1) * width + k)] - shift for k in range(width)]
                    sums = tuple(s + jnp.exp2(t - m) for s, t, m in zip(sums, terms, largest))
                if taking:
                    terms = [s_ref[r, lane(chunk * width + k)] - shift for k in range(width)]
                    maxes = tuple(jnp.maximum(m, t) for m, t in zip(maxes, terms))
            return sums, maxes

        sums, maxes = lax.fori_loop(
            0, steps, step, ((zero,) * width if summing else (), (low,) * width if taking else ())
        )
        for k in range(width if summing else 0):
            most = jnp.max(largest[k], axis=0, keepdims=True)
            total = jnp.sum(sums[k] * jnp.exp2(largest[k] - most), axis=0, keepdims=True)
            at = (chunk - 1) * width + k
            col_ref[at : at + 1, :] = most + jnp.log2(total)
        largest = maxes


def first_row_kernel(*refs):
    count = 9
    sources, refs = refs[:count], refs[count:]
    s_ref, out_ref = refs[:2]
    held, (lhs_ref, cp_ref, max_ref, sum_ref, sems) = refs[2 : 2 + count], refs[2 + count :]
    copies = [
        pltpu.make_async_copy(source, target, sems.at[i])
        for i, (source, target) in enumerate(zip(sources, held))
    ]
    for copy in copies:
        copy.start()
    fw_ref, ff_ref, sp_ref, start_ref = held[:4]
    copies[0].wait()
    copies[2].wait()
    rank, cols = ff_ref.shape
    mixed = lax.dot_general(
        sp_ref[...], fw_ref[...], (((0,), (0,)), ((), ())), precision=HIGHEST,
        preferred_element_type=jnp.float32,
    ) * LOG2E

    def split(value):
        first = value.astype(jnp.bfloat16)
        rest = value - first.astype(jnp.float32)
        second = rest.astype(jnp.bfloat16)
        third = (rest - second.astype(jnp.float32)).astype(jnp.bfloat16)
        return first, second, third

    m1, m2, m3 = split(mixed)
    stacked = jnp.concatenate([m.astype(jnp.float32) for m in (m1, m2, m1, m2, m3, m1)], axis=0)
    lhs_ref[...] = stacked.T.astype(jnp.bfloat16)
    copies[1].wait()
    width = math.gcd(cols, 512)
    copies[3].wait()
    cp_ref[...] = start_ref[...] * LOG2E

    def dot_step(c):
        chunk = pl.ds(c * width, width)
        f1, f2, f3 = split(ff_ref[:, chunk])
        rhs = jnp.concatenate([f1, f1, f2, f2, f1, f3], axis=0)
        s_ref[:, chunk] = lax.dot_general(
            lhs_ref[...], rhs, (((1,), (0,)), ((), ())), preferred_element_type=jnp.float32
        )

    tiles = width // LANES
    rows = s_ref.shape[0]
    for c in range(cols // width + 1):
        if c < cols // width:
            dot_step(c)
        if c:
            row_lse_chunk(s_ref, cp_ref, max_ref, sum_ref, (c - 1) * tiles, tiles, range(rows // GROUP), c > 1)
    row_lse_end(max_ref, sum_ref, out_ref)
    for copy in copies[4:]:
        copy.wait()


def damped(old, log, mass):
    return 0.5 * old + 0.5 * (log - mass * LOG2E)


def col_kernel_of(parts, first):
    def kernel(*refs):
        s_ref, part_refs = refs[0], refs[1 : 1 + parts]
        old_ref, mass_ref, out_ref, log_ref, pot_ref, wide_ref, col_ref = refs[1 + parts :]
        log = lse_parts([p[...] for p in part_refs])
        old = old_ref[...] * LOG2E if first else old_ref[...]
        pot = damped(old, log, mass_ref[...])
        log_ref[...] = log
        pot_ref[...] = pot
        spread_rows(pot, wide_ref)
        col_lse(s_ref, wide_ref, col_ref)
        send_all(col_ref, out_ref)

    return kernel


def row_kernel_of(first):
    def kernel(s_ref, got_ref, old_ref, mass_ref, out_ref, log_ref, pot_ref, max_ref, sum_ref):
        log = lse_parts([got_ref[p] for p in range(got_ref.shape[0])])
        old = old_ref[...] * LOG2E if first else old_ref[...]
        log_ref[...] = log
        pot_ref[...] = damped(old, log, mass_ref[...])
        row_lse(s_ref, pot_ref, max_ref, sum_ref, out_ref)

    return kernel


def col_adjoint_pass(s_ref, wide_ref, log_ref, weight_ref, total_ref, acc_in, acc_out, out_ref):
    rows, cols = s_ref.shape
    tiles = cols // LANES
    per_step = math.gcd(rows // GROUP, 4)

    def group_step(g, carry):
        rs = [pl.ds(g * (GROUP * per_step) + q * GROUP, GROUP) for q in range(per_step)]
        shifts = [wide_ref[r, :] for r in rs]
        totals = [None] * per_step
        for k in range(tiles):
            log = log_ref[k : k + 1, :]
            weight = weight_ref[k : k + 1, :]
            for q in range(per_step):
                value = jnp.exp2(s_ref[rs[q], lane(k)] - shifts[q] - log) * weight
                totals[q] = value if totals[q] is None else totals[q] + value
                kept = value if acc_in is None else acc_in[rs[q], lane(k)] + value
                acc_out[rs[q], lane(k)] = kept
        for q in range(per_step):
            total_ref[rs[q], :] = totals[q]
        return carry

    lax.fori_loop(0, rows // (GROUP * per_step), group_step, 0)
    for block in range(rows // LANES):
        part = total_ref[pl.ds(block * LANES, LANES), :].T
        out_ref[block : block + 1, :] = jnp.sum(part, axis=0, keepdims=True)


def last_col_adjoint_kernel(s_ref, got_ref, cot_ref, pot_ref, acc_ref, out_ref, half_ref, wide_ref, total_ref, log_ref):
    log_ref[...] = lse_parts([got_ref[p] for p in range(got_ref.shape[0])])
    half_ref[...] = 0.5 * cot_ref[...]
    spread_rows(pot_ref[...], wide_ref)
    col_adjoint_pass(s_ref, wide_ref, log_ref, half_ref, total_ref, None, acc_ref, out_ref)


def col_adjoint_kernel(s_ref, acc_in, got_ref, half_in, pot_ref, log_ref, acc_ref, out_ref, half_ref, wide_ref, total_ref):
    summed = tree([got_ref[p] for p in range(got_ref.shape[0])], jnp.add)
    half_ref[...] = 0.5 * (half_in[...] - summed)
    spread_rows(pot_ref[...], wide_ref)
    col_adjoint_pass(s_ref, wide_ref, log_ref, half_ref, total_ref, acc_in, acc_ref, out_ref)


def row_adjoint_pass(s_ref, pot_ref, log_wide, weight_wide, acc_in, acc_out, col_ref):
    rows, cols = s_ref.shape
    width, chunks = col_blocking(cols, 8)
    per_step = math.gcd(rows // GROUP, 8)

    for c in range(chunks):
        first = c * width
        pots = [wide_lane(pot_ref, first + k) for k in range(width)]

        def row_step(step, totals):
            for q in range(per_step):
                r = pl.ds(step * (GROUP * per_step) + q * GROUP, GROUP)
                log = log_wide[r, :]
                weight = weight_wide[r, :]
                fresh = []
                for k in range(width):
                    value = jnp.exp2(s_ref[r, lane(first + k)] - pots[k] - log) * weight
                    acc_out[r, lane(first + k)] = acc_in[r, lane(first + k)] + value
                    fresh.append(totals[k] + value)
                totals = tuple(fresh)
            return totals

        zero = jnp.zeros((GROUP, LANES), jnp.float32)
        totals = lax.fori_loop(0, rows // (GROUP * per_step), row_step, (zero,) * width)
        for k in range(width):
            col_ref[first + k : first + k + 1, :] = jnp.sum(totals[k], axis=0, keepdims=True)


def row_adjoint_kernel_of(parts, last):
    def kernel(*refs):
        s_ref, acc_in = refs[:2]
        part_refs = refs[2 : 2 + parts]
        rest = refs[2 + parts :]
        half_in, pot_ref, log_ref = rest[:3]
        rest = rest[3:]
        if last:
            fw_ref, ff_ref, out_ref, half_ref, acc_ref, log_wide, weight_wide, col_ref, pot_scaled = rest
            pot_scaled[...] = pot_ref[...] * LOG2E
            pot_ref = pot_scaled
        else:
            acc_ref, out_ref, half_ref, log_wide, weight_wide, col_ref = rest
        summed = tree([p[...] for p in part_refs], jnp.add)
        half = 0.5 * (half_in[...] - summed)
        half_ref[...] = half
        spread_rows(log_ref[...], log_wide)
        spread_rows(half, weight_wide)
        row_adjoint_pass(s_ref, pot_ref, log_wide, weight_wide, acc_in, acc_ref, col_ref)
        if not last:
            send_all(col_ref, out_ref)
            return
        grad = contract(acc_ref, fw_ref, ff_ref)
        col_rows = col_ref.shape[0]
        value = col_ref[...]
        for peer in range(out_ref.shape[0]):
            out_ref[peer, :col_rows, :] = value
            out_ref[peer, col_rows:, :] = grad

    return kernel


def contract(acc_ref, fw_ref, ff_ref):
    rows, cols = acc_ref.shape
    rank = ff_ref.shape[0]
    width = math.gcd(cols, 512)

    def halves(value):
        first = value.astype(jnp.bfloat16)
        return first, (value - first.astype(jnp.float32)).astype(jnp.bfloat16)

    w1, w2 = halves(fw_ref[...])
    left = jnp.concatenate([w1, w2], axis=0)
    left = jnp.concatenate([left, left], axis=1)

    def dot_step(c, grad):
        chunk = pl.ds(c * width, width)
        weights = jnp.concatenate(halves(acc_ref[:, chunk]), axis=0)
        rows_done = jnp.dot(left, weights, preferred_element_type=jnp.float32)
        rows_done = rows_done[:rank] + rows_done[rank:]
        return grad + lax.dot_general(
            jnp.concatenate(halves(rows_done), axis=0),
            jnp.concatenate(halves(ff_ref[:, chunk]), axis=0),
            (((1,), (1,)), ((), ())), preferred_element_type=jnp.float32,
        )

    zero = jnp.zeros((2 * rank, 2 * rank), jnp.float32)
    grad = lax.fori_loop(0, cols // width, dot_step, zero)
    grad = grad[:rank] + grad[rank:]
    both = grad + pltpu.roll(grad, rank, 1)
    half = rank // 2
    lanes = lax.broadcasted_iota(jnp.int32, (half, 2 * rank), 1)
    return jnp.where(lanes < rank, both[:half], both[half:])


def unfold_kernel(*refs):
    grad = tree([ref[...] for ref in refs[:-1]], jnp.add)
    half, lanes = grad.shape
    rank = lanes // 2
    refs[-1][:half, :] = grad[:, :rank]
    refs[-1][half:, :] = pltpu.roll(grad, rank, 1)[:, :rank]


def peers_of(part, axis):
    size = lax.axis_size(axis)
    if size & (size - 1):
        gathered = lax.all_gather(part, axis)
        return [gathered[i] for i in range(size)]
    return [part] + [
        lax.ppermute(part, axis, [(i, i ^ d) for i in range(size)]) for d in range(1, size)
    ]


def exchange_cols(block):
    return lax.all_to_all(block, "wrk", 0, 0, tiled=True)


def body(feat_wrk, feat_firm, surplus, row_start, col_start, row_mass, col_mass, row_cot, col_cot):
    rows, rank = feat_wrk.shape
    cols = feat_firm.shape[1]
    wrk, firm = lax.axis_size("wrk"), lax.axis_size("firm")
    row_dims = (rows // LANES, LANES)
    col_dims = (cols // LANES, LANES)
    row_start, row_mass, row_cot = (a.reshape(row_dims) for a in (row_start, row_mass, row_cot))
    col_start, col_mass, col_cot = (a.reshape(col_dims) for a in (col_start, col_mass, col_cot))
    wide = pltpu.VMEM((rows, LANES), jnp.float32)
    col_vec = pltpu.VMEM(col_dims, jnp.float32)
    row_out, col_out = shape_of(*row_dims), shape_of(*col_dims)
    send_out = shape_of(wrk, *col_dims)
    acc_out = shape_of(rows, cols)

    inputs = (feat_wrk.T, feat_firm, surplus, col_start, row_start, row_mass, col_mass, row_cot, col_cot)
    inputs = tuple(pltpu.with_memory_space_constraint(a, pltpu.HBM) for a in inputs)
    scores, part, *held = call(
        first_row_kernel, "row_first", (acc_out, row_out, *(shape_of(*a.shape) for a in inputs)), inputs,
        (
            pltpu.VMEM((rows, 6 * rank), jnp.bfloat16), col_vec, wide, wide,
            pltpu.SemaphoreType.DMA((len(inputs),)),
        ),
        pltpu.HBM,
    )
    feat_wrk, feat_firm, surplus, col_start, row_start, row_mass, col_mass, row_cot, col_cot = held
    row_pots, col_pots, row_logs, col_logs = [row_start], [col_start], [], []
    for t in range(ITERS):
        parts = peers_of(part, "firm")
        block, log, pot = call(
            col_kernel_of(len(parts), t == 0), f"col_{t}", (send_out, row_out, row_out),
            (scores, *parts, row_pots[-1], row_mass), (wide, col_vec),
        )
        row_logs.append(log)
        row_pots.append(pot)
        got = exchange_cols(block)
        if t == ITERS - 1:
            break
        part, log, pot = call(
            row_kernel_of(t == 0), f"row_{t + 1}", (row_out, col_out, col_out),
            (scores, got, col_pots[-1], col_mass), (wide, wide),
        )
        col_logs.append(log)
        col_pots.append(pot)

    acc, part, col_half = call(
        last_col_adjoint_kernel, f"col_adj_{ITERS - 1}", (acc_out, row_out, col_out),
        (scores, got, col_cot, row_pots[ITERS]), (wide, wide, col_vec),
    )
    row_half = row_cot
    for t in reversed(range(ITERS)):
        parts = peers_of(part, "firm")
        args = (scores, acc, *parts, row_half, col_pots[t], row_logs[t])
        if t == 0:
            break
        acc, block, row_half = call(
            row_adjoint_kernel_of(len(parts), False), f"row_adj_{t}", (acc_out, send_out, row_out),
            args, (wide, wide, col_vec),
        )
        got = exchange_cols(block)
        acc, part, col_half = call(
            col_adjoint_kernel, f"col_adj_{t - 1}", (acc_out, row_out, col_out),
            (scores, acc, got, col_half, row_pots[t], col_logs[t - 1]), (wide, wide),
        )

    grad_rows = rank * rank // LANES
    block, row_half = call(
        row_adjoint_kernel_of(len(parts), True), "row_adj_0",
        (shape_of(wrk, col_dims[0] + grad_rows, LANES), row_out),
        (*args, feat_wrk, feat_firm),
        (pltpu.VMEM((rows, cols), jnp.float32), wide, wide, col_vec, col_vec),
    )
    summed = jnp.sum(exchange_cols(block), axis=0)
    col_bar = (col_half - summed[: col_dims[0]]).reshape(cols)
    summed = summed[col_dims[0] :]
    grad_surplus = call(
        unfold_kernel, "unfold", shape_of(rank, rank), peers_of(summed, "firm")
    )
    return (grad_surplus, row_half.reshape(rows), col_bar)


def solution(mesh):
    return jax.shard_map(
        body,
        mesh=mesh,
        in_specs=(
            P("wrk", None),
            P(None, "firm"),
            P(),
            P("wrk"),
            P("firm"),
            P("wrk"),
            P("firm"),
            P("wrk"),
            P("firm"),
        ),
        out_specs=(P(), P("wrk"), P("firm")),
        check_vma=False,
    )
```

```python
import math

import jax
import jax.numpy as jnp
from jax import lax
from jax.experimental import pallas as pl
from jax.experimental.pallas import tpu as pltpu
from jax.sharding import PartitionSpec as P

ITERS = 3
LOG2E = 1.0 / math.log(2.0)
HIGHEST = lax.Precision.HIGHEST
LANES = 128
GROUP = 8
WHOLE = pl.BlockSpec(memory_space=pltpu.VMEM)
VMEM_LIMIT = 14 * 1024 * 1024


def tree(values, combine):
    values = list(values)
    while len(values) > 1:
        paired = [combine(values[i], values[i + 1]) for i in range(0, len(values) - 1, 2)]
        if len(values) % 2:
            paired.append(values[-1])
        values = paired
    return values[0]


def shape_of(*dims):
    return jax.ShapeDtypeStruct(dims, jnp.float32)


def call(kernel, name, outs, args, scratch=(), space=pltpu.VMEM):
    return pl.pallas_call(
        kernel,
        name=name,
        out_shape=outs,
        in_specs=[pl.BlockSpec(memory_space=space)] * len(args),
        out_specs=jax.tree.map(lambda _: WHOLE, outs),
        scratch_shapes=scratch,
        compiler_params=pltpu.CompilerParams(vmem_limit_bytes=VMEM_LIMIT),
    )(*args)


def lane(k):
    return pl.ds(k * LANES, LANES)


def lse_parts(parts):
    largest = tree(parts, jnp.maximum)
    return largest + jnp.log2(tree([jnp.exp2(p - largest) for p in parts], jnp.add))


def spread_rows(value, ref):
    for block in range(value.shape[0]):
        wide = jnp.broadcast_to(value[block : block + 1, :], (LANES, LANES))
        ref[pl.ds(block * LANES, LANES), :] = wide.T


def row_lse_chunk(s_ref, shift_ref, max_ref, sum_ref, first, width, groups, later):
    shifts = [wide_lane(shift_ref, first + k) for k in range(width)]
    for g in groups:
        r = pl.ds(g * GROUP, GROUP)
        terms = [s_ref[r, lane(first + k)] - shifts[k] for k in range(width)]
        largest = tree(terms, jnp.maximum)
        if later:
            before = max_ref[r, :]
            largest = jnp.maximum(largest, before)
        total = tree([jnp.exp2(t - largest) for t in terms], jnp.add)
        if later:
            total = total + sum_ref[r, :] * jnp.exp2(before - largest)
        max_ref[r, :] = largest
        sum_ref[r, :] = total


def row_lse_end(max_ref, sum_ref, out_ref):
    for block in range(max_ref.shape[0] // LANES):
        b = pl.ds(block * LANES, LANES)
        maxes = max_ref[b, :].T
        sums = sum_ref[b, :].T
        largest = jnp.max(maxes, axis=0, keepdims=True)
        total = jnp.sum(sums * jnp.exp2(maxes - largest), axis=0, keepdims=True)
        out_ref[block : block + 1, :] = largest + jnp.log2(total)


def row_lse(s_ref, shift_ref, max_ref, sum_ref, out_ref):
    rows, cols = s_ref.shape
    width, chunks = col_blocking(cols, 8)
    per_step = math.gcd(rows // GROUP, 8)
    for chunk in range(chunks):

        def step(i, carry):
            groups = [i * per_step + q for q in range(per_step)]
            row_lse_chunk(s_ref, shift_ref, max_ref, sum_ref, chunk * width, width, groups, chunk > 0)
            return carry

        lax.fori_loop(0, rows // (GROUP * per_step), step, 0)
    row_lse_end(max_ref, sum_ref, out_ref)


def col_blocking(cols, most):
    tiles = cols // LANES
    width = math.gcd(tiles, most)
    return width, tiles // width


def wide_lane(ref, k):
    return jnp.broadcast_to(ref[k : k + 1, :], (GROUP, LANES))


def send_all(col_ref, out_ref):
    value = col_ref[...]
    for peer in range(out_ref.shape[0]):
        out_ref[peer] = value


def col_lse(s_ref, shift_ref, col_ref):
    rows, cols = s_ref.shape
    width, chunks = col_blocking(cols, 8)
    per_step = math.gcd(rows // GROUP, 8)
    steps = rows // (GROUP * per_step)
    low = jnp.full((GROUP, LANES), -jnp.inf, jnp.float32)
    zero = jnp.zeros((GROUP, LANES), jnp.float32)
    largest = None
    for chunk in range(chunks + 1):
        summing, taking = chunk > 0, chunk < chunks

        def step(i, carry):
            sums, maxes = carry
            for q in range(per_step):
                r = pl.ds(i * (GROUP * per_step) + q * GROUP, GROUP)
                shift = shift_ref[r, :]
                if summing:
                    terms = [s_ref[r, lane((chunk - 1) * width + k)] - shift for k in range(width)]
                    sums = tuple(s + jnp.exp2(t - m) for s, t, m in zip(sums, terms, largest))
                if taking:
                    terms = [s_ref[r, lane(chunk * width + k)] - shift for k in range(width)]
                    maxes = tuple(jnp.maximum(m, t) for m, t in zip(maxes, terms))
            return sums, maxes

        sums, maxes = lax.fori_loop(
            0, steps, step, ((zero,) * width if summing else (), (low,) * width if taking else ())
        )
        for k in range(width if summing else 0):
            most = jnp.max(largest[k], axis=0, keepdims=True)
            total = jnp.sum(sums[k] * jnp.exp2(largest[k] - most), axis=0, keepdims=True)
            at = (chunk - 1) * width + k
            col_ref[at : at + 1, :] = most + jnp.log2(total)
        largest = maxes


def first_row_kernel(*refs):
    count = 9
    sources, refs = refs[:count], refs[count:]
    s_ref, out_ref = refs[:2]
    held, (lhs_ref, cp_ref, max_ref, sum_ref, sems) = refs[2 : 2 + count], refs[2 + count :]
    copies = [
        pltpu.make_async_copy(source, target, sems.at[i])
        for i, (source, target) in enumerate(zip(sources, held))
    ]
    for copy in copies:
        copy.start()
    fw_ref, ff_ref, sp_ref, start_ref = held[:4]
    copies[0].wait()
    copies[2].wait()
    rank, cols = ff_ref.shape
    mixed = lax.dot_general(
        sp_ref[...], fw_ref[...], (((0,), (0,)), ((), ())), precision=HIGHEST,
        preferred_element_type=jnp.float32,
    ) * LOG2E

    def split(value):
        first = value.astype(jnp.bfloat16)
        rest = value - first.astype(jnp.float32)
        second = rest.astype(jnp.bfloat16)
        third = (rest - second.astype(jnp.float32)).astype(jnp.bfloat16)
        return first, second, third

    m1, m2, m3 = split(mixed)
    stacked = jnp.concatenate([m.astype(jnp.float32) for m in (m1, m2, m1, m2, m3, m1)], axis=0)
    lhs_ref[...] = stacked.T.astype(jnp.bfloat16)
    copies[1].wait()
    width = math.gcd(cols, 512)
    copies[3].wait()
    cp_ref[...] = start_ref[...] * LOG2E

    def dot_step(c):
        chunk = pl.ds(c * width, width)
        f1, f2, f3 = split(ff_ref[:, chunk])
        rhs = jnp.concatenate([f1, f1, f2, f2, f1, f3], axis=0)
        s_ref[:, chunk] = lax.dot_general(
            lhs_ref[...], rhs, (((1,), (0,)), ((), ())), preferred_element_type=jnp.float32
        )

    tiles = width // LANES
    rows = s_ref.shape[0]
    for c in range(cols // width + 1):
        if c < cols // width:
            dot_step(c)
        if c:
            row_lse_chunk(s_ref, cp_ref, max_ref, sum_ref, (c - 1) * tiles, tiles, range(rows // GROUP), c > 1)
    row_lse_end(max_ref, sum_ref, out_ref)
    for copy in copies[4:]:
        copy.wait()


def damped(old, log, mass):
    return 0.5 * old + 0.5 * (log - mass * LOG2E)


def col_kernel_of(parts, first):
    def kernel(*refs):
        s_ref, part_refs = refs[0], refs[1 : 1 + parts]
        old_ref, mass_ref, out_ref, log_ref, pot_ref, wide_ref, col_ref = refs[1 + parts :]
        log = lse_parts([p[...] for p in part_refs])
        old = old_ref[...] * LOG2E if first else old_ref[...]
        pot = damped(old, log, mass_ref[...])
        log_ref[...] = log
        pot_ref[...] = pot
        spread_rows(pot, wide_ref)
        col_lse(s_ref, wide_ref, col_ref)
        send_all(col_ref, out_ref)

    return kernel


def row_kernel_of(first):
    def kernel(s_ref, got_ref, old_ref, mass_ref, out_ref, log_ref, pot_ref, max_ref, sum_ref):
        log = lse_parts([got_ref[p] for p in range(got_ref.shape[0])])
        old = old_ref[...] * LOG2E if first else old_ref[...]
        log_ref[...] = log
        pot_ref[...] = damped(old, log, mass_ref[...])
        row_lse(s_ref, pot_ref, max_ref, sum_ref, out_ref)

    return kernel


def col_adjoint_pass(s_ref, wide_ref, log_ref, weight_ref, total_ref, acc_in, acc_out, out_ref):
    rows, cols = s_ref.shape
    tiles = cols // LANES
    per_step = math.gcd(rows // GROUP, 4)

    def group_step(g, carry):
        rs = [pl.ds(g * (GROUP * per_step) + q * GROUP, GROUP) for q in range(per_step)]
        shifts = [wide_ref[r, :] for r in rs]
        totals = [None] * per_step
        for k in range(tiles):
            log = log_ref[k : k + 1, :]
            weight = weight_ref[k : k + 1, :]
            for q in range(per_step):
                value = jnp.exp2(s_ref[rs[q], lane(k)] - shifts[q] - log) * weight
                totals[q] = value if totals[q] is None else totals[q] + value
                kept = value if acc_in is None else acc_in[rs[q], lane(k)] + value
                acc_out[rs[q], lane(k)] = kept
        for q in range(per_step):
            total_ref[rs[q], :] = totals[q]
        return carry

    lax.fori_loop(0, rows // (GROUP * per_step), group_step, 0)
    for block in range(rows // LANES):
        part = total_ref[pl.ds(block * LANES, LANES), :].T
        out_ref[block : block + 1, :] = jnp.sum(part, axis=0, keepdims=True)


def last_col_adjoint_kernel(s_ref, got_ref, cot_ref, pot_ref, acc_ref, out_ref, half_ref, wide_ref, total_ref, log_ref):
    log_ref[...] = lse_parts([got_ref[p] for p in range(got_ref.shape[0])])
    half_ref[...] = 0.5 * cot_ref[...]
    spread_rows(pot_ref[...], wide_ref)
    col_adjoint_pass(s_ref, wide_ref, log_ref, half_ref, total_ref, None, acc_ref, out_ref)


def col_adjoint_kernel(s_ref, acc_in, got_ref, half_in, pot_ref, log_ref, acc_ref, out_ref, half_ref, wide_ref, total_ref):
    summed = tree([got_ref[p] for p in range(got_ref.shape[0])], jnp.add)
    half_ref[...] = 0.5 * (half_in[...] - summed)
    spread_rows(pot_ref[...], wide_ref)
    col_adjoint_pass(s_ref, wide_ref, log_ref, half_ref, total_ref, acc_in, acc_ref, out_ref)


def row_adjoint_pass(s_ref, pot_ref, log_wide, weight_wide, acc_in, acc_out, col_ref):
    rows, cols = s_ref.shape
    width, chunks = col_blocking(cols, 8)
    per_step = math.gcd(rows // GROUP, 8)

    for c in range(chunks):
        first = c * width
        pots = [wide_lane(pot_ref, first + k) for k in range(width)]

        def row_step(step, totals):
            for q in range(per_step):
                r = pl.ds(step * (GROUP * per_step) + q * GROUP, GROUP)
                log = log_wide[r, :]
                weight = weight_wide[r, :]
                fresh = []
                for k in range(width):
                    value = jnp.exp2(s_ref[r, lane(first + k)] - pots[k] - log) * weight
                    acc_out[r, lane(first + k)] = acc_in[r, lane(first + k)] + value
                    fresh.append(totals[k] + value)
                totals = tuple(fresh)
            return totals

        zero = jnp.zeros((GROUP, LANES), jnp.float32)
        totals = lax.fori_loop(0, rows // (GROUP * per_step), row_step, (zero,) * width)
        for k in range(width):
            col_ref[first + k : first + k + 1, :] = jnp.sum(totals[k], axis=0, keepdims=True)


def row_adjoint_kernel_of(parts, last):
    def kernel(*refs):
        s_ref, acc_in = refs[:2]
        part_refs = refs[2 : 2 + parts]
        rest = refs[2 + parts :]
        half_in, pot_ref, log_ref = rest[:3]
        rest = rest[3:]
        if last:
            fw_ref, ff_ref, out_ref, half_ref, acc_ref, log_wide, weight_wide, col_ref, pot_scaled = rest
            pot_scaled[...] = pot_ref[...] * LOG2E
            pot_ref = pot_scaled
        else:
            acc_ref, out_ref, half_ref, log_wide, weight_wide, col_ref = rest
        summed = tree([p[...] for p in part_refs], jnp.add)
        half = 0.5 * (half_in[...] - summed)
        half_ref[...] = half
        spread_rows(log_ref[...], log_wide)
        spread_rows(half, weight_wide)
        row_adjoint_pass(s_ref, pot_ref, log_wide, weight_wide, acc_in, acc_ref, col_ref)
        if not last:
            send_all(col_ref, out_ref)
            return
        grad = contract(acc_ref, fw_ref, ff_ref)
        col_rows = col_ref.shape[0]
        value = col_ref[...]
        for peer in range(out_ref.shape[0]):
            out_ref[peer, :col_rows, :] = value
            out_ref[peer, col_rows:, :] = grad

    return kernel


def contract(acc_ref, fw_ref, ff_ref):
    rows, cols = acc_ref.shape
    rank = ff_ref.shape[0]
    width = math.gcd(cols, 512)

    def halves(value):
        first = value.astype(jnp.bfloat16)
        return first, (value - first.astype(jnp.float32)).astype(jnp.bfloat16)

    w1, w2 = halves(fw_ref[...])
    left = jnp.concatenate([w1, w2], axis=0)
    left = jnp.concatenate([left, left], axis=1)

    def dot_step(c, grad):
        chunk = pl.ds(c * width, width)
        weights = jnp.concatenate(halves(acc_ref[:, chunk]), axis=0)
        rows_done = jnp.dot(left, weights, preferred_element_type=jnp.float32)
        rows_done = rows_done[:rank] + rows_done[rank:]
        return grad + lax.dot_general(
            jnp.concatenate(halves(rows_done), axis=0),
            jnp.concatenate(halves(ff_ref[:, chunk]), axis=0),
            (((1,), (1,)), ((), ())), preferred_element_type=jnp.float32,
        )

    zero = jnp.zeros((2 * rank, 2 * rank), jnp.float32)
    grad = lax.fori_loop(0, cols // width, dot_step, zero)
    grad = grad[:rank] + grad[rank:]
    both = grad + pltpu.roll(grad, rank, 1)
    half = rank // 2
    lanes = lax.broadcasted_iota(jnp.int32, (half, 2 * rank), 1)
    return jnp.where(lanes < rank, both[:half], both[half:])


def unfold_kernel(*refs):
    col_half_ref, summed_ref, *part_refs, grad_ref, col_ref = refs
    col_ref[...] = col_half_ref[...] - summed_ref[: col_ref.shape[0], :]
    grad = tree([ref[...] for ref in part_refs], jnp.add)
    half, lanes = grad.shape
    rank = lanes // 2
    grad_ref[:half, :] = grad[:, :rank]
    grad_ref[half:, :] = pltpu.roll(grad, rank, 1)[:, :rank]


def peers_of(part, axis):
    size = lax.axis_size(axis)
    if size & (size - 1):
        gathered = lax.all_gather(part, axis)
        return [gathered[i] for i in range(size)]
    return [part] + [
        lax.ppermute(part, axis, [(i, i ^ d) for i in range(size)]) for d in range(1, size)
    ]


def exchange_cols(block):
    return lax.all_to_all(block, "wrk", 0, 0, tiled=True)


def body(feat_wrk, feat_firm, surplus, row_start, col_start, row_mass, col_mass, row_cot, col_cot):
    rows, rank = feat_wrk.shape
    cols = feat_firm.shape[1]
    wrk, firm = lax.axis_size("wrk"), lax.axis_size("firm")
    row_dims = (rows // LANES, LANES)
    col_dims = (cols // LANES, LANES)
    row_start, row_mass, row_cot = (a.reshape(row_dims) for a in (row_start, row_mass, row_cot))
    col_start, col_mass, col_cot = (a.reshape(col_dims) for a in (col_start, col_mass, col_cot))
    wide = pltpu.VMEM((rows, LANES), jnp.float32)
    col_vec = pltpu.VMEM(col_dims, jnp.float32)
    row_out, col_out = shape_of(*row_dims), shape_of(*col_dims)
    send_out = shape_of(wrk, *col_dims)
    acc_out = shape_of(rows, cols)

    inputs = (feat_wrk.T, feat_firm, surplus, col_start, row_start, row_mass, col_mass, row_cot, col_cot)
    inputs = tuple(pltpu.with_memory_space_constraint(a, pltpu.HBM) for a in inputs)
    scores, part, *held = call(
        first_row_kernel, "row_first", (acc_out, row_out, *(shape_of(*a.shape) for a in inputs)), inputs,
        (
            pltpu.VMEM((rows, 6 * rank), jnp.bfloat16), col_vec, wide, wide,
            pltpu.SemaphoreType.DMA((len(inputs),)),
        ),
        pltpu.HBM,
    )
    feat_wrk, feat_firm, surplus, col_start, row_start, row_mass, col_mass, row_cot, col_cot = held
    row_pots, col_pots, row_logs, col_logs = [row_start], [col_start], [], []
    for t in range(ITERS):
        parts = peers_of(part, "firm")
        block, log, pot = call(
            col_kernel_of(len(parts), t == 0), f"col_{t}", (send_out, row_out, row_out),
            (scores, *parts, row_pots[-1], row_mass), (wide, col_vec),
        )
        row_logs.append(log)
        row_pots.append(pot)
        got = exchange_cols(block)
        if t == ITERS - 1:
            break
        part, log, pot = call(
            row_kernel_of(t == 0), f"row_{t + 1}", (row_out, col_out, col_out),
            (scores, got, col_pots[-1], col_mass), (wide, wide),
        )
        col_logs.append(log)
        col_pots.append(pot)

    acc, part, col_half = call(
        last_col_adjoint_kernel, f"col_adj_{ITERS - 1}", (acc_out, row_out, col_out),
        (scores, got, col_cot, row_pots[ITERS]), (wide, wide, col_vec),
    )
    row_half = row_cot
    for t in reversed(range(ITERS)):
        parts = peers_of(part, "firm")
        args = (scores, acc, *parts, row_half, col_pots[t], row_logs[t])
        if t == 0:
            break
        acc, block, row_half = call(
            row_adjoint_kernel_of(len(parts), False), f"row_adj_{t}", (acc_out, send_out, row_out),
            args, (wide, wide, col_vec),
        )
        got = exchange_cols(block)
        acc, part, col_half = call(
            col_adjoint_kernel, f"col_adj_{t - 1}", (acc_out, row_out, col_out),
            (scores, acc, got, col_half, row_pots[t], col_logs[t - 1]), (wide, wide),
        )

    grad_rows = rank * rank // LANES
    block, row_half = call(
        row_adjoint_kernel_of(len(parts), True), "row_adj_0",
        (shape_of(wrk, col_dims[0] + grad_rows, LANES), row_out),
        (*args, feat_wrk, feat_firm),
        (pltpu.VMEM((rows, cols), jnp.float32), wide, wide, col_vec, col_vec),
    )
    summed = jnp.sum(exchange_cols(block), axis=0)
    grad_surplus, col_bar = call(
        unfold_kernel, "unfold", (shape_of(rank, rank), col_out),
        (col_half, summed, *peers_of(summed[col_dims[0] :], "firm")),
    )
    return (grad_surplus, row_half.reshape(rows), col_bar.reshape(cols))


def solution(mesh):
    return jax.shard_map(
        body,
        mesh=mesh,
        in_specs=(
            P("wrk", None),
            P(None, "firm"),
            P(),
            P("wrk"),
            P("firm"),
            P("wrk"),
            P("firm"),
            P("wrk"),
            P("firm"),
        ),
        out_specs=(P(), P("wrk"), P("firm")),
        check_vma=False,
    )
```
